32 devices in a mesh: tok: 8 (over z, x), head: 4 (over y, core).
Axes of the slice: x: 2, y: 2, z: 4, core: 2. Of those that a mesh axis runs over, the one named last changes fastest.
Arguments:
- single: bfloat16 [256, 768], P('tok'), may hold values from -6 to 6
- pair: bfloat16 [256, 256, 128], P('tok', 'head'), may hold values from -161 to 161
- atoms: bfloat16 [6144, 128], P('tok'), may hold values from -60 to 60
- atom_counts: int32 [256], P('tok'), may hold values from 4 to 24, as said below
- w_atom: bfloat16 [128, 3, 128], P(None, None, 'head'), may hold values from -0.5 to 0.5
- w_atom_token: bfloat16 [128, 768], P('head'), may hold values from -6 to 6
- ln_gain: bfloat16 [768], replicated, may hold values from 0.099609375 to 1.8984375
- w_proj: bfloat16 [768, 4, 768], P(None, None, 'head'), may hold values from -0.21875 to 0.21875
- w_pair_bias: bfloat16 [128, 16], replicated, may hold values from -3.5 to 3.5
- w_out: bfloat16 [768, 768], P('head'), may hold values from -0.21875 to 0.21875
- ln_gain2: bfloat16 [768], replicated, may hold values from 0.099609375 to 1.8984375
- w_trans: bfloat16 [768, 2, 1536], P(None, None, 'head'), may hold values from -0.21875 to 0.21875
- w_trans_out: bfloat16 [1536, 768], P('head'), may hold values from -0.15625 to 0.15625
Outputs:
- refined: bfloat16 [256, 768], P('tok', 'head')
- atom_mix: bfloat16 [128, 6144], P('head', 'tok')
The draws below stay inside these ranges and needn't reach their ends.
Inputs may be any that keep to these rules, and one draw needn't show every extreme that they name: `atom_counts`: every token has 4 to 24 atoms; in every draw all tokens of some group of 32 have 24 atoms.
All inputs are finite; a program needn't handle non-finite values.
Results may differ from the reference program's by a relative error of at most 0.013.
Values may be sent and summed in bfloat16 or wider, within the bound.
A program may use at most 64 MiB of HBM per device.

```python
import jax
import jax.numpy as jnp
from jax import lax

D = 768
H = 16
CZ = 128
ATOM_WIDTH = 128
AH = 4
FF = 1536
TOK_DEV = 32
QWIN = 32
KWIN = 128
MINA = 4
MAXA = 24
NTOK = 256
ACAP = 768
SLOTS_TOTAL = 6144


def draw_atom_counts(key, part):
    group_list = NTOK // TOK_DEV
    level_key = jax.random.fold_in(key, 11)
    token_key = jax.random.fold_in(key, 12)
    full_key = jax.random.fold_in(key, 13)
    levels = jax.random.randint(level_key, (group_list, 1), MINA, MAXA + 1)
    random_bits = jax.random.randint(token_key, (group_list, TOK_DEV), 0, 1 << 20)
    counts = MINA + random_bits % (levels - MINA + 1)
    full_group = jax.random.randint(full_key, (), 0, group_list)
    counts = jnp.where(jnp.arange(group_list)[:, None] == full_group, MAXA, counts)
    return counts.reshape(NTOK).astype(jnp.int32)


def draw_pair(key, part):
    starting_key = jax.random.fold_in(key, 21)
    value_entries = jnp.clip(jax.random.normal(starting_key, (NTOK, NTOK, CZ), jnp.float32), -6.0, 6.0)
    return value_entries.astype(jnp.bfloat16)


def draw_atoms(key, part):
    starting_key = jax.random.fold_in(key, 31)
    value_entries = jnp.clip(jax.random.normal(starting_key, (SLOTS_TOTAL, ATOM_WIDTH), jnp.float32), -6.0, 6.0)
    return value_entries.astype(jnp.bfloat16)


def steps_of(own_key, shape, pieces, smallest, high):
    level, own = 1.0, jax.random.fold_in(own_key, 6)
    for position, blocks in pieces:
        heights = jnp.exp(jax.random.uniform(jax.random.fold_in(own, position), (blocks,), jnp.float32, smallest / len(pieces), high / len(pieces)))
        level = level * jnp.repeat(heights, shape[position] // blocks).reshape([-1 if axis == position else 1 for axis in range(len(shape))])
    return level


def bell_draw(rng, shape, deviation, limit, shards=(), held_as=jnp.bfloat16):
    values = deviation * jax.random.normal(rng, shape, jnp.float32)
    if shards:
        values = values * steps_of(rng, shape, shards, -0.22, 0.18)
    return jnp.clip(values, -limit, limit).astype(held_as)


def setup_inputs(seed: int = 0) -> dict:
    splits = jax.random.split(jax.random.key(seed), 14)
    return {
        "single": bell_draw(splits[0], (NTOK, D), 1.0, 6.0, ((0, 8),)),
        "pair": draw_pair(jax.random.fold_in(splits[13], 71), 0),
        "atoms": draw_atoms(jax.random.fold_in(splits[13], 71), 0),
        "atom_counts": draw_atom_counts(jax.random.fold_in(splits[13], 71), 0),
        "w_atom": bell_draw(splits[4], (ATOM_WIDTH, 3, ATOM_WIDTH), ATOM_WIDTH ** -0.5, 0.5, ((2, 4),)),
        "w_atom_token": bell_draw(splits[5], (ATOM_WIDTH, D), 1.0, 6.0, ((0, 4),)),
        "ln_gain": jnp.clip(1.0 + 0.18 * jax.random.normal(splits[6], (D,), jnp.float32), 0.099609375, 1.8984375).astype(jnp.bfloat16),
        "w_proj": bell_draw(splits[7], (D, 4, D), D ** -0.5, 0.21875, ((2, 4),)),
        "w_pair_bias": bell_draw(splits[8], (CZ, H), 0.22, 3.5),
        "w_out": bell_draw(splits[9], (D, D), D ** -0.5, 0.21875, ((0, 4),)),
        "ln_gain2": jnp.clip(1.0 + 0.18 * jax.random.normal(splits[10], (D,), jnp.float32), 0.099609375, 1.8984375).astype(jnp.bfloat16),
        "w_trans": bell_draw(splits[11], (D, 2, FF), D ** -0.5, 0.21875, ((2, 4),)),
        "w_trans_out": bell_draw(splits[12], (FF, D), FF ** -0.5, 0.15625, ((0, 4),)),
    }


norm_eps = 1e-05
masked_value = -1000000000.0

def layer_norm(value_entries, gain):
    average = lax.optimization_barrier(jnp.mean(value_entries, axis=-1, keepdims=True))
    centred = value_entries - average
    spread = lax.optimization_barrier(jnp.mean(centred * centred, axis=-1, keepdims=True))
    return centred * lax.rsqrt(spread + norm_eps) * gain.astype(jnp.float32)

def group_layout(atom_counts):
    counts = atom_counts.reshape(NTOK // TOK_DEV, TOK_DEV).astype(jnp.int32)
    starts = (jnp.cumsum(counts, axis=1) - counts).astype(jnp.int32)
    totals = lax.optimization_barrier(jnp.sum(counts, axis=1)).astype(jnp.int32)
    return (counts, starts, totals)

def atom_attention(atoms, atom_counts, w_atom):
    group_list = NTOK // TOK_DEV
    windows = ACAP // QWIN
    head_size = ATOM_WIDTH // AH
    tail_rows = (KWIN - QWIN) // 2
    counts, starts, totals = group_layout(atom_counts)
    start_offsets = (jnp.cumsum(totals) - totals).astype(jnp.int32)
    everything = jnp.sum(totals).astype(jnp.int32)
    projected_rows = jnp.dot(atoms, w_atom.reshape(ATOM_WIDTH, 3 * ATOM_WIDTH), preferred_element_type=jnp.float32).astype(jnp.bfloat16)
    slot_position = jnp.arange(SLOTS_TOTAL, dtype=jnp.int32)
    owning_group = slot_position // ACAP
    inner_position = slot_position % ACAP
    active_mask = inner_position < totals[owning_group]
    atom_position = jnp.where(active_mask, start_offsets[owning_group] + inner_position, SLOTS_TOTAL).astype(jnp.int32)
    packed_rows = jnp.zeros((SLOTS_TOTAL, 2 * ATOM_WIDTH), jnp.bfloat16).at[atom_position].set(projected_rows[:, ATOM_WIDTH:], mode='drop')

    def single_group(group_pos):
        block = lax.dynamic_slice_in_dim(projected_rows, group_pos * ACAP, ACAP, 0)
        queries = block[:, :ATOM_WIDTH].reshape(windows, QWIN, AH, head_size).astype(jnp.float32)
        local_pos = jnp.arange(windows, dtype=jnp.int32)[:, None] * QWIN + jnp.arange(KWIN, dtype=jnp.int32)[None, :] - tail_rows
        target_index = start_offsets[group_pos] + local_pos
        key_valid = (target_index >= 0) & (target_index < everything)
        loaded_rows = packed_rows[jnp.clip(target_index, 0, SLOTS_TOTAL - 1)]
        key_rows = loaded_rows[:, :, :ATOM_WIDTH].reshape(windows, KWIN, AH, head_size).astype(jnp.float32)
        value_rows = loaded_rows[:, :, ATOM_WIDTH:].reshape(windows, KWIN, AH, head_size).astype(jnp.float32)
        scores = jnp.einsum('wqhd,wkhd->whqk', queries, key_rows) * head_size ** (-0.5)
        scores = jnp.where(key_valid[:, None, None, :], scores, masked_value)
        row_max = lax.optimization_barrier(jnp.max(scores, axis=-1, keepdims=True))
        lifted = jnp.exp(scores - row_max)
        weights = (lifted / lax.optimization_barrier(jnp.sum(lifted, axis=-1, keepdims=True))).astype(jnp.bfloat16)
        mixed = jnp.einsum('whqk,wkhd->wqhd', weights.astype(jnp.float32), value_rows)
        query_live = (jnp.arange(ACAP, dtype=jnp.int32) < totals[group_pos]).reshape(windows, QWIN)
        mixed = jnp.where(query_live[:, :, None, None], mixed, 0.0)
        return mixed.reshape(ACAP, ATOM_WIDTH).astype(jnp.bfloat16)
    return lax.map(single_group, jnp.arange(group_list, dtype=jnp.int32)).reshape(SLOTS_TOTAL, ATOM_WIDTH)

def token_means(atom_out, atom_counts):
    group_list = NTOK // TOK_DEV
    counts, starts, totals = group_layout(atom_counts)
    slot_position = jnp.arange(ACAP, dtype=jnp.int32)
    member = (slot_position[None, None, :] >= starts[:, :, None]) & (slot_position[None, None, :] < (starts + counts)[:, :, None])
    member = member.astype(jnp.float32)
    totals_rows = jnp.einsum('gts,gsc->gtc', member, atom_out.reshape(group_list, ACAP, ATOM_WIDTH).astype(jnp.float32))
    return (totals_rows / counts[:, :, None].astype(jnp.float32)).reshape(NTOK, ATOM_WIDTH)

def reference(single, pair, atoms, atom_counts, w_atom, w_atom_token, ln_gain, w_proj, w_pair_bias, w_out, ln_gain2, w_trans, w_trans_out):
    atom_out = atom_attention(atoms, atom_counts, w_atom)
    token_atoms = token_means(atom_out, atom_counts).astype(jnp.bfloat16)
    residual_state = single.astype(jnp.float32) + jnp.dot(token_atoms, w_atom_token, preferred_element_type=jnp.float32)
    normed = layer_norm(residual_state, ln_gain).astype(jnp.bfloat16)
    projected_rows = jnp.dot(normed, w_proj.reshape(D, 4 * D), preferred_element_type=jnp.float32).reshape(NTOK, 4, D)
    queries = projected_rows[:, 0].astype(jnp.bfloat16)
    key_rows = projected_rows[:, 1].astype(jnp.bfloat16)
    value_rows = projected_rows[:, 2].astype(jnp.bfloat16)
    gate_raw = projected_rows[:, 3]
    pair_term = jnp.dot(pair.reshape(NTOK * NTOK, CZ), w_pair_bias, preferred_element_type=jnp.float32).astype(jnp.bfloat16)
    pair_term = jnp.transpose(pair_term.reshape(NTOK, NTOK, H), (2, 0, 1))
    head_size = D // H

    def one_head(head_pos):
        query_head = lax.dynamic_slice_in_dim(queries, head_pos * head_size, head_size, 1)
        key_head = lax.dynamic_slice_in_dim(key_rows, head_pos * head_size, head_size, 1)
        value_head = lax.dynamic_slice_in_dim(value_rows, head_pos * head_size, head_size, 1)
        pair_head = lax.dynamic_index_in_dim(pair_term, head_pos, 0, keepdims=False)
        scores = jnp.dot(query_head, key_head.T, preferred_element_type=jnp.float32) * head_size ** (-0.5)
        scores = scores + pair_head.astype(jnp.float32)
        row_max = lax.optimization_barrier(jnp.max(scores, axis=-1, keepdims=True))
        lifted = jnp.exp(scores - row_max)
        weights = (lifted / lax.optimization_barrier(jnp.sum(lifted, axis=-1, keepdims=True))).astype(jnp.bfloat16)
        return jnp.dot(weights, value_head, preferred_element_type=jnp.float32)
    context = lax.map(one_head, jnp.arange(H, dtype=jnp.int32))
    context = jnp.transpose(context, (1, 0, 2)).reshape(NTOK, D)
    gated_rows = (context * jax.nn.sigmoid(gate_raw)).astype(jnp.bfloat16)
    state_after = residual_state + jnp.dot(gated_rows, w_out, preferred_element_type=jnp.float32)
    normed_after = layer_norm(state_after, ln_gain2).astype(jnp.bfloat16)
    gate_up = jnp.dot(normed_after, w_trans.reshape(D, 2 * FF), preferred_element_type=jnp.float32)
    hidden = (jax.nn.silu(gate_up[:, :FF]) * gate_up[:, FF:]).astype(jnp.bfloat16)
    refined = (state_after + jnp.dot(hidden, w_trans_out, preferred_element_type=jnp.float32)).astype(jnp.bfloat16)
    return (refined, atom_out.T)
```

```python
import functools

import jax
import jax.numpy as jnp
from jax import lax
from jax.experimental import pallas as pl
from jax.experimental.pallas import tpu as pltpu
from jax.sharding import PartitionSpec as P

H = 16
AH = 4
QWIN = 32
KWIN = 128
TAIL = (KWIN - QWIN) // 2
LEAD = (KWIN + QWIN) // 2
MESH = pl.DeviceIdType.MESH
f32 = jnp.float32
bf16 = jnp.bfloat16

norm_eps = 1e-05
masked_value = -1000000000.0
GROUP = 4
FRONT = 2 * QWIN
EDGE = 3
FRONT = 2 * QWIN
EDGE = 3
FRONT = 2 * QWIN
EDGE = 3
FRONT = 2 * QWIN
EDGE = 3
FRONT = 2 * QWIN
EDGE = 3
VMEM_MIB = 58


def dot(a, b):
    return jnp.dot(a, b, preferred_element_type=f32)


def dot_t(a, b):
    return lax.dot_general(a, b, (((1,), (1,)), ((), ())), preferred_element_type=f32)


def iota(shape, dim):
    return lax.broadcasted_iota(jnp.int32, shape, dim)


def eye(n):
    return (iota((n, n), 0) == iota((n, n), 1)).astype(bf16)


def layer_norm(x, gain):
    average = jnp.mean(x, axis=-1, keepdims=True)
    centred = x - average
    spread = jnp.mean(centred * centred, axis=-1, keepdims=True)
    return centred * lax.rsqrt(spread + norm_eps) * gain.astype(f32)


def total_wait(ref, sem):
    pltpu.make_async_copy(ref, ref, sem).wait()


def total_wait(ref, sem):
    pltpu.make_async_copy(ref, ref, sem).wait()


def total_wait(ref, sem):
    pltpu.make_async_copy(ref, ref, sem).wait()


def total_wait(ref, sem):
    pltpu.make_async_copy(ref, ref, sem).wait()


def total_wait(ref, sem):
    pltpu.make_async_copy(ref, ref, sem).wait()


def kernel(
    nt,
    nh,
    single_hbm,
    pair_hbm,
    atoms_hbm,
    counts_hbm,
    w_atom_hbm,
    w_tok_hbm,
    gain1_hbm,
    w_proj_hbm,
    w_pair_hbm,
    w_out_hbm,
    gain2_hbm,
    w_trans_hbm,
    w_down_hbm,
    refined,
    atom_mix,
    counts,
    single,
    atoms,
    w_atom,
    w_tok,
    gain1,
    gain2,
    w_pair,
    pair,
    w_proj,
    w_out,
    w_raw,
    w_gate,
    w_up,
    w_down,
    local_sem,
    tail,
    halo,
    halo_s,
    halo_r,
    sg,
    sg_s,
    sg_r,
    fwd_s,
    fwd_r,
    wt,
    wt_s,
    wt_r,
    pair_f,
    pair_s,
    pair_r,
    pb_s,
    pb_r,
    queries,
    keys,
    values,
    inner,
    mixed,
    ta,
    ta_s,
    ta_r,
    parts,
    part_s,
    part_r,
    fin_s_buf,
    fin_r_buf,
    own_buf,
    fin_s,
    fin_r,
):
    t = lax.axis_index("tok")
    h = lax.axis_index("head")
    rows, width = single.shape
    slots = atoms.shape[0]
    awidth = w_atom.shape[1]
    heads = w_pair.shape[0]
    local_heads = heads // nh
    lw = w_proj.shape[1]
    hd = lw // local_heads
    kblock = pair.shape[1]
    half = width // 2
    hidden_width = w_gate.shape[1]

    barrier = pltpu.get_barrier_semaphore()
    head_peers = [lax.rem(h + o, nh) for o in range(nh)]

    def everyone(act):
        for peer in head_peers[1:]:
            act(t, peer)

        def step(o, c):
            other = lax.rem(t + o, nt)
            for peer in head_peers:
                act(other, peer)
            return c

        lax.fori_loop(1, nt, step, 0)

    everyone(
        lambda pt, ph: pl.semaphore_signal(barrier, inc=1, device_id=(pt, ph), device_id_type=MESH)
    )

    locals_ = [
        pltpu.make_async_copy(src, dst, local_sem.at[i])
        for i, (src, dst) in enumerate(
            [
                (atoms_hbm, atoms),
                (counts_hbm, counts),
                (w_atom_hbm, w_atom),
                (single_hbm, single),
                (w_tok_hbm, w_tok),
                (w_pair_hbm, w_pair),
                (pair_hbm, pair),
                (w_trans_hbm, w_raw),
                (w_proj_hbm, w_proj),
                (gain1_hbm, gain1),
                (w_out_hbm, w_out),
                (gain2_hbm, gain2),
                (w_down_hbm, w_down),
            ]
        )
    ]
    for copy in locals_:
        copy.start()

    locals_[1].wait()
    cnt_row = counts[...].astype(f32)
    live = jnp.sum(cnt_row, axis=1, keepdims=True).astype(jnp.int32)
    locals_[0].wait()

    @pl.when(t < nt - 1)
    def _():
        pick = iota((TAIL, slots), 1) == iota((TAIL, slots), 0) + (live - TAIL)
        tail[...] = dot(pick.astype(bf16), atoms[...]).astype(bf16)

    c_half = lax.rem(h, 2)
    locals_[3].wait()
    locals_[4].wait()
    sg[c_half, pl.ds(pl.multiple_of(t * rows, rows), rows), :] = single[
        :, pl.ds(pl.multiple_of(c_half * half, 128), half)
    ]
    wt[h] = w_tok[...]

    pl.semaphore_wait(barrier, nt * nh - 1)

    nxt = lax.rem(t + 1, nt)
    prv = lax.rem(t + nt - 1, nt)
    up = pltpu.make_async_remote_copy(
        tail, halo.at[pl.ds(0, TAIL)], halo_s.at[0], halo_r.at[0], device_id=(nxt, h), device_id_type=MESH
    )
    down = pltpu.make_async_remote_copy(
        atoms.at[pl.ds(0, LEAD)],
        halo.at[pl.ds(TAIL, LEAD)],
        halo_s.at[1],
        halo_r.at[1],
        device_id=(prv, h),
        device_id_type=MESH,
    )
    down.start()
    up.start()

    def head_send(src_of, dst, s, r):
        for peer in head_peers[1:]:
            pltpu.make_async_remote_copy(
                src_of(peer), dst.at[h], s, r, device_id=(t, peer), device_id_type=MESH
            ).start()

    def head_wait(ref, sem):
        total_wait(ref.at[pl.ds(0, nh - 1)], sem)

    own_rows = pl.ds(pl.multiple_of(t * rows, rows), rows)

    def start_sg(o, c):
        block = sg.at[c_half, own_rows, :]
        pltpu.make_async_remote_copy(
            block, block, sg_s, sg_r, device_id=(lax.rem(t + o, nt), h), device_id_type=MESH
        ).start()
        return c

    lax.fori_loop(1, nt, start_sg, 0)
    head_send(lambda peer: wt.at[h], wt, wt_s, wt_r)

    ri = iota((rows, rows), 0)
    ci = iota((rows, rows), 1)
    cnt_b = jnp.broadcast_to(cnt_row, (rows, rows))
    cnt_col = jnp.sum(jnp.where(ri == ci, cnt_b, 0.0), axis=1, keepdims=True)
    end_col = jnp.sum(jnp.where(ci <= ri, cnt_b, 0.0), axis=1, keepdims=True)
    end_i = end_col.astype(jnp.int32)
    start_i = (end_col - cnt_col).astype(jnp.int32)
    last = (live - 1) // QWIN
    r0 = (last - (EDGE - 1)) * QWIN

    locals_[2].wait()
    queries[...] = dot_t(atoms[...], w_atom[0]).astype(bf16)
    for ref, i in ((keys, 1), (values, 2)):
        ref[TAIL : TAIL + slots, :awidth] = dot_t(atoms[...], w_atom[i]).astype(bf16)
        ref[0:TAIL, :awidth] = jnp.zeros((TAIL, awidth), bf16)
        ref[TAIL + slots :, :awidth] = jnp.zeros((LEAD, awidth), bf16)
    values[:, awidth:] = jnp.ones((values.shape[0], values.shape[1] - awidth), bf16)

    locals_[5].wait()
    locals_[6].wait()
    for i in range(rows):
        pair_f[:, i, :] = dot_t(w_pair[...], pair[i])
    for p in range(nh):
        pair_s[p] = pair_f[p * local_heads : (p + 1) * local_heads].astype(bf16)
    pair_r[h] = pair_s[h]
    head_send(lambda peer: pair_s.at[peer], pair_r, pb_s, pb_r)

    scale = awidth ** (-0.5)
    qrows = GROUP * QWIN
    krows = qrows + KWIN
    lane = iota((1, krows), 1)
    first = iota((qrows, krows), 0) // QWIN * QWIN
    lanes = iota((qrows, krows), 1)
    band = jnp.where((lanes >= first) & (lanes < first + KWIN), 0.0, masked_value)
    wide_lane = iota((qrows, KWIN), 1)
    for w in range(slots // qrows):
        a = w * qrows
        pos = lane + (a - TAIL)
        outside = jnp.where((pos >= 0) & (pos < live), 0.0, masked_value)
        s = dot_t(queries[a : a + qrows], keys[a : a + krows, :]) * scale + (band + outside)
        top = jnp.max(s, axis=-1, keepdims=True)
        e = jnp.exp(s - top).astype(bf16)
        pv = dot(e, values[a : a + krows, :])
        inner[a : a + qrows] = jnp.where(wide_lane < 2 * awidth, pv, top)
        mixed[a : a + qrows] = (pv[:, :awidth] / pv[:, awidth : awidth + 1]).astype(bf16)

    slot = iota((rows, slots), 1)
    member = (slot >= start_i) & (slot < end_i)
    inside = member & (slot >= FRONT) & ((slot < r0) | (slot >= r0 + EDGE * QWIN))
    sums = dot(inside.astype(bf16), mixed[...])
    erow = iota((rows, FRONT + EDGE * QWIN), 1)
    eslot = jnp.where(erow < FRONT, erow, erow - FRONT + r0)
    touched = (eslot >= start_i) & (eslot < end_i) & ((erow < FRONT) | (eslot >= FRONT))
    touched = touched.astype(bf16)

    nrow = FRONT + EDGE * QWIN
    qi = iota((nrow, KWIN), 0)
    ki = iota((nrow, KWIN), 1)
    seen_prev = (qi < FRONT) & (ki < TAIL) & (ki >= qi // QWIN * QWIN) & (t > 0)
    reach = (qi - FRONT) // QWIN * QWIN + r0 + LEAD - live
    seen_next = (qi >= FRONT) & (ki >= TAIL) & (ki - TAIL < reach) & (t < nt - 1)
    edge_mask = jnp.where(seen_prev | seen_next, 0.0, masked_value)
    pick = iota((EDGE * QWIN, slots), 1) == iota((EDGE * QWIN, slots), 0) + r0
    a_edge = dot(pick.astype(bf16), atoms[...]).astype(bf16)
    a_edge = jnp.concatenate([atoms[0:FRONT], a_edge], axis=0)
    q_edge = dot_t(a_edge, w_atom[0]).astype(bf16)
    in_edge = jnp.dot(pick.astype(f32), inner[...], precision=lax.Precision.HIGHEST, preferred_element_type=f32)
    in_edge = jnp.concatenate([inner[0:FRONT], in_edge], axis=0)
    top_in = in_edge[:, 2 * awidth : 2 * awidth + 1]

    locals_[7].wait()
    woven = w_raw[...].reshape(2 * width, hidden_width)
    blk = 128
    si = iota((blk, 2 * blk), 0)
    sj = iota((blk, 2 * blk), 1)
    picks = [(sj == 2 * si + p).astype(bf16) for p in (0, 1)]
    for b in range(width // blk):
        for p, ref in enumerate((w_gate, w_up)):
            ref[b * blk : (b + 1) * blk] = dot(picks[p], woven[2 * b * blk : 2 * (b + 1) * blk]).astype(bf16)

    up.wait_recv()
    down.wait_recv()
    kh = dot_t(halo[...], w_atom[1]).astype(bf16)
    vh = dot_t(halo[...], w_atom[2]).astype(bf16)
    vh = jnp.concatenate([vh, jnp.ones((KWIN, KWIN - awidth), bf16)], axis=1)
    s = dot_t(q_edge, kh) * scale + edge_mask
    top_out = jnp.max(s, axis=-1, keepdims=True)
    e = jnp.exp(s - top_out).astype(bf16)
    pv = dot(e, vh)
    top = jnp.maximum(top_in, top_out)
    pv = jnp.exp(top_in - top) * in_edge + jnp.exp(top_out - top) * pv
    edge = (pv[:, :awidth] / pv[:, awidth : awidth + 1]).astype(bf16)
    means = (sums + dot(touched, edge)) / cnt_col
    packs = KWIN // awidth
    prow = rows // packs
    packed = jnp.concatenate([means[i * prow : (i + 1) * prow] for i in range(packs)], axis=1)
    ta[h, t] = packed.astype(bf16)

    def ta_send(pt, ph):
        block = ta.at[h, t]
        pltpu.make_async_remote_copy(
            block, block, ta_s, ta_r, device_id=(pt, ph), device_id_type=MESH
        ).start()

    everyone(ta_send)

    at_window = iota((QWIN, awidth), 0) // QWIN
    for w in range(slots // QWIN):
        a = w * QWIN
        if a < FRONT:
            mixed[a : a + QWIN] = edge[a : a + QWIN]
        else:
            block = mixed[a : a + QWIN].astype(f32)
            for i in range(EDGE):
                b = FRONT + i * QWIN
                here = at_window + (w + EDGE - 1 - i) == last
                block = jnp.where(here, edge[b : b + QWIN].astype(f32), block)
            mixed[a : a + QWIN] = block.astype(bf16)
    alive = iota((slots, 1), 0) < live
    mix = jnp.where(alive, mixed[...].astype(f32), 0.0).astype(bf16)
    atom_mix[...] = dot_t(eye(awidth), mix).astype(bf16)

    total_wait(sg.at[0, pl.ds(0, (nt - 1) * rows), :], sg_r)
    partner = h + 1 - 2 * c_half
    fwd = pltpu.make_async_remote_copy(
        sg.at[c_half], sg.at[c_half], fwd_s, fwd_r, device_id=(t, partner), device_id_type=MESH
    )
    fwd.start()
    head_wait(wt, wt_r)
    head_wait(pair_r, pb_r)
    for i in range(8, 13):
        locals_[i].wait()
    fwd.wait_recv()
    flat_ta = ta.reshape(nh * nt, prow, packs * awidth).at[pl.ds(0, nh * nt - 1)]
    total_wait(flat_ta, ta_r)

    own = single[...].astype(f32)
    full = jnp.concatenate([sg[0], sg[1]], axis=1).astype(f32)
    at_lane = iota((1, packs * awidth), 1)

    def spread(x):
        x = x.astype(f32)
        return [
            jnp.where((at_lane >= i * awidth) & (at_lane < (i + 1) * awidth), x, 0.0)
            for i in range(packs)
        ]

    lhs = jnp.concatenate(
        [
            jnp.concatenate([m.reshape(nt, 1, prow, packs * awidth) for m in spread(ta[p].astype(f32).reshape(nt * prow, packs * awidth))], axis=1)
            .reshape(nt * rows, packs * awidth)
            .astype(bf16)
            for p in range(nh)
        ],
        axis=1,
    )
    own_lhs = jnp.concatenate(
        [jnp.concatenate(spread(ta[p, t]), axis=0).astype(bf16) for p in range(nh)], axis=1
    )
    wide = jnp.concatenate([wt[p] for p in range(nh) for i in range(packs)], axis=0)
    term = dot(lhs, wide)
    own_term = dot(own_lhs, wide)
    state = own + own_term
    normed_own = layer_norm(state, gain1[...].reshape(1, width)).astype(bf16)
    normed = layer_norm(full + term, gain1[...].reshape(1, width)).astype(bf16)
    q = dot_t(normed_own, w_proj[0])
    k = dot_t(normed, w_proj[1]).astype(bf16)
    v = dot_t(normed, w_proj[2]).astype(bf16)
    gate = jax.nn.sigmoid(dot_t(normed_own, w_proj[3]))
    col = iota((1, lw), 1)
    in_head = [(col >= hd * i) & (col < hd * (i + 1)) for i in range(local_heads)]
    stacked = jnp.concatenate([jnp.where(m, q, 0.0) for m in in_head], axis=0).astype(bf16)
    s = dot_t(stacked, k) * hd ** (-0.5)
    bias = jnp.concatenate(
        [pair_r[p].astype(f32).reshape(local_heads * rows, kblock) for p in range(nh)], axis=1
    )
    s = s + bias
    e = jnp.exp(s - jnp.max(s, axis=-1, keepdims=True))
    p_ = (e / jnp.sum(e, axis=-1, keepdims=True)).astype(bf16)
    ctx = dot(p_, v)
    context = jnp.zeros((rows, lw), f32)
    for i, m in enumerate(in_head):
        context = jnp.where(m, ctx[i * rows : (i + 1) * rows], context)
    gated = (context * gate).astype(bf16)
    parts[h] = dot(gated, w_out[...]).astype(bf16)
    head_send(lambda peer: parts.at[h], parts, part_s, part_r)

    up.wait_send()
    down.wait_send()
    fwd.wait_send()
    head_wait(wt, wt_s)
    head_wait(pair_r, pb_s)
    total_wait(sg.at[0, pl.ds(0, (nt - 1) * rows), :], sg_s)
    total_wait(flat_ta, ta_s)

    head_wait(parts, part_r)
    total = parts[0].astype(f32)
    for p in range(1, nh):
        total += parts[p].astype(f32)
    after = state + total
    normed_after = layer_norm(after, gain2[...].reshape(1, width)).astype(bf16)
    g = dot(normed_after, w_gate[...])
    u = dot(normed_after, w_up[...])
    hidden = (jax.nn.silu(g) * u).astype(bf16)
    update = dot(hidden, w_down[...])
    quarter = width // nh
    for p in range(nh):
        fin_s_buf[p] = update[:, p * quarter : (p + 1) * quarter].astype(bf16)
    head_send(lambda peer: fin_s_buf.at[peer], fin_r_buf, fin_s, fin_r)
    for p in range(nh):
        own_buf[p] = after[:, p * quarter : (p + 1) * quarter]
    acc = own_buf[h] + fin_s_buf[h].astype(f32)
    fin_r_buf[h] = jnp.zeros((rows, quarter), bf16)
    head_wait(parts, part_s)
    head_wait(fin_r_buf, fin_s)
    head_wait(fin_r_buf, fin_r)
    for p in range(nh):
        acc += fin_r_buf[p].astype(f32)
    refined[...] = acc.astype(bf16)


def deliver(refined_in, mix_in, refined, atom_mix, sem):
    copies = [
        pltpu.make_async_copy(refined_in, refined, sem.at[0]),
        pltpu.make_async_copy(mix_in, atom_mix, sem.at[1]),
    ]
    for copy in copies:
        copy.start()
    for copy in copies:
        copy.wait()


def shards(
    nt,
    nh,
    single,
    pair,
    atoms,
    atom_counts,
    w_atom,
    w_atom_token,
    ln_gain,
    w_proj,
    w_pair_bias,
    w_out,
    ln_gain2,
    w_trans,
    w_trans_out,
):
    rows, width = single.shape
    slots, channels = atoms.shape
    awidth = w_atom.shape[2]
    heads = w_pair_bias.shape[1]
    local_heads = heads // nh
    kblock = pair.shape[1]
    n = nt * nh
    lw = w_proj.shape[2]
    hidden = w_trans.shape[2]
    quarter = width // nh
    vm = pl.BlockSpec(memory_space=pltpu.VMEM)
    hbm = pl.BlockSpec(memory_space=pltpu.HBM)
    dma = pltpu.SemaphoreType.DMA
    vmem = pltpu.VMEM
    refined, atom_mix = pl.pallas_call(
        functools.partial(kernel, nt, nh),
        out_shape=(vmem((rows, quarter), bf16), vmem((awidth, slots), bf16)),
        in_specs=[hbm] * 13,
        out_specs=(vm, vm),
        scratch_shapes=[
            vmem((1, rows), jnp.int32),
            vmem(single.shape, bf16),
            vmem(atoms.shape, bf16),
            vmem((3, awidth, channels), bf16),
            vmem(w_atom_token.shape, bf16),
            vmem(ln_gain.shape, bf16),
            vmem(ln_gain2.shape, bf16),
            vmem((heads, pair.shape[2]), bf16),
            vmem(pair.shape, bf16),
            vmem((4, lw, width), bf16),
            vmem(w_out.shape, bf16),
            vmem(w_trans.shape, bf16),
            vmem((width, hidden), bf16),
            vmem((width, hidden), bf16),
            vmem(w_trans_out.shape, bf16),
            dma((13,)),
            vmem((TAIL, channels), bf16),
            vmem((KWIN, channels), bf16),
            dma((2,)),
            dma((2,)),
            vmem((2, nt * rows, width // 2), bf16),
            dma,
            dma,
            dma,
            dma,
            vmem((nh, awidth, width), bf16),
            dma,
            dma,
            vmem((heads, rows, kblock), f32),
            vmem((nh, local_heads, rows, kblock), bf16),
            vmem((nh, local_heads, rows, kblock), bf16),
            dma,
            dma,
            vmem((slots, awidth), bf16),
            vmem((TAIL + slots + LEAD, awidth), bf16),
            vmem((TAIL + slots + LEAD, KWIN), bf16),
            vmem((slots, KWIN), f32),
            vmem((slots, awidth), bf16),
            vmem((nh, nt, rows * awidth // KWIN, KWIN), bf16),
            dma,
            dma,
            vmem((nh, rows, width), bf16),
            dma,
            dma,
            vmem((nh, rows, quarter), bf16),
            vmem((nh, rows, quarter), bf16),
            vmem((nh, rows, quarter), f32),
            dma,
            dma,
        ],
        compiler_params=pltpu.CompilerParams(
            collective_id=0, has_side_effects=True, vmem_limit_bytes=VMEM_MIB * 1024 * 1024
        ),
        name="step",
    )(
        single,
        pair,
        atoms,
        atom_counts.reshape(1, rows),
        jnp.transpose(w_atom, (1, 2, 0)),
        w_atom_token,
        ln_gain,
        jnp.transpose(w_proj, (1, 2, 0)),
        w_pair_bias.T,
        w_out,
        ln_gain2,
        w_trans,
        w_trans_out,
    )
    return pl.pallas_call(
        deliver,
        out_shape=(
            jax.ShapeDtypeStruct((rows, quarter), bf16),
            jax.ShapeDtypeStruct((awidth, slots), bf16),
        ),
        in_specs=[vm, vm],
        out_specs=(hbm, hbm),
        scratch_shapes=[dma((2,))],
        name="deliver",
    )(
        pltpu.with_memory_space_constraint(refined, pltpu.VMEM),
        pltpu.with_memory_space_constraint(atom_mix, pltpu.VMEM),
    )


def solution(mesh):
    return jax.shard_map(
        functools.partial(shards, mesh.shape["tok"], mesh.shape["head"]),
        mesh=mesh,
        in_specs=(
            P("tok", None),
            P("tok", "head", None),
            P("tok", None),
            P("tok"),
            P(None, None, "head"),
            P("head", None),
            P(),
            P(None, None, "head"),
            P(),
            P("head", None),
            P(),
            P(None, None, "head"),
            P("head", None),
        ),
        out_specs=(P("tok", "head"), P("head", "tok")),
        check_vma=False,
    )
```

```python
import functools

import jax
import jax.numpy as jnp
from jax import lax
from jax.experimental import pallas as pl
from jax.experimental.pallas import tpu as pltpu
from jax.sharding import PartitionSpec as P

H = 16
AH = 4
QWIN = 32
KWIN = 128
TAIL = (KWIN - QWIN) // 2
LEAD = (KWIN + QWIN) // 2
MESH = pl.DeviceIdType.MESH
f32 = jnp.float32
bf16 = jnp.bfloat16

norm_eps = 1e-05
masked_value = -1000000000.0
GROUP = 4
FRONT = 2 * QWIN
EDGE = 3
FRONT = 2 * QWIN
EDGE = 3
FRONT = 2 * QWIN
EDGE = 3
FRONT = 2 * QWIN
EDGE = 3
FRONT = 2 * QWIN
EDGE = 3
VMEM_MIB = 58


def dot(a, b):
    return jnp.dot(a, b, preferred_element_type=f32)


def dot_t(a, b):
    return lax.dot_general(a, b, (((1,), (1,)), ((), ())), preferred_element_type=f32)


def iota(shape, dim):
    return lax.broadcasted_iota(jnp.int32, shape, dim)


def eye(n):
    return (iota((n, n), 0) == iota((n, n), 1)).astype(bf16)


def layer_norm(x, gain):
    average = jnp.mean(x, axis=-1, keepdims=True)
    centred = x - average
    spread = jnp.mean(centred * centred, axis=-1, keepdims=True)
    return centred * lax.rsqrt(spread + norm_eps) * gain.astype(f32)


def total_wait(ref, sem):
    pltpu.make_async_copy(ref, ref, sem).wait()


def total_wait(ref, sem):
    pltpu.make_async_copy(ref, ref, sem).wait()


def total_wait(ref, sem):
    pltpu.make_async_copy(ref, ref, sem).wait()


def total_wait(ref, sem):
    pltpu.make_async_copy(ref, ref, sem).wait()


def total_wait(ref, sem):
    pltpu.make_async_copy(ref, ref, sem).wait()


def kernel(
    nt,
    nh,
    single_hbm,
    pair_hbm,
    atoms_hbm,
    counts_hbm,
    w_atom_hbm,
    w_tok_hbm,
    gain1_hbm,
    w_proj_hbm,
    w_pair_hbm,
    w_out_hbm,
    gain2_hbm,
    w_trans_hbm,
    w_down_hbm,
    refined,
    atom_mix,
    counts,
    single,
    atoms,
    w_atom,
    w_tok,
    gain1,
    gain2,
    w_pair,
    pair,
    w_proj,
    w_out,
    w_raw,
    w_gate,
    w_up,
    w_down,
    local_sem,
    tail,
    halo,
    halo_s,
    halo_r,
    sg,
    sg_s,
    sg_r,
    fwd_s,
    fwd_r,
    wt,
    wt_s,
    wt_r,
    pair_f,
    pair_s,
    pair_r,
    pb_s,
    pb_r,
    queries,
    keys,
    values,
    inner,
    mixed,
    ta,
    ta_s,
    ta_r,
    parts,
    part_s,
    part_r,
    fin_s_buf,
    fin_r_buf,
    own_buf,
    fin_s,
    fin_r,
):
    t = lax.axis_index("tok")
    h = lax.axis_index("head")
    rows, width = single.shape
    slots = atoms.shape[0]
    awidth = w_atom.shape[1]
    heads = w_pair.shape[0]
    local_heads = heads // nh
    lw = w_proj.shape[1]
    hd = lw // local_heads
    kblock = pair.shape[1]
    half = width // 2
    hidden_width = w_gate.shape[1]

    barrier = pltpu.get_barrier_semaphore()
    head_peers = [lax.rem(h + o, nh) for o in range(nh)]

    def everyone(act, sign):
        def step(o, c):
            other = lax.rem(t + sign * o + nt, nt)
            for peer in head_peers:
                act(other, peer)
            return c

        lax.fori_loop(1, nt, step, 0)
        for peer in head_peers[1:]:
            act(t, peer)

    everyone(
        lambda pt, ph: pl.semaphore_signal(barrier, inc=1, device_id=(pt, ph), device_id_type=MESH),
        -1,
    )

    locals_ = [
        pltpu.make_async_copy(src, dst, local_sem.at[i])
        for i, (src, dst) in enumerate(
            [
                (atoms_hbm, atoms),
                (counts_hbm, counts),
                (w_atom_hbm, w_atom),
                (single_hbm, single),
                (w_tok_hbm, w_tok),
                (w_pair_hbm, w_pair),
                (pair_hbm, pair),
                (w_trans_hbm, w_raw),
                (w_proj_hbm, w_proj),
                (gain1_hbm, gain1),
                (w_out_hbm, w_out),
                (gain2_hbm, gain2),
                (w_down_hbm, w_down),
            ]
        )
    ]
    for copy in locals_:
        copy.start()

    locals_[1].wait()
    cnt_row = counts[...].astype(f32)
    live = jnp.sum(cnt_row, axis=1, keepdims=True).astype(jnp.int32)
    locals_[0].wait()

    has_next = t < nt - 1
    has_prev = t > 0

    @pl.when(has_next)
    def _():
        pick = iota((TAIL, slots), 1) == iota((TAIL, slots), 0) + (live - TAIL)
        tail[...] = dot(pick.astype(bf16), atoms[...]).astype(bf16)

    pl.semaphore_wait(barrier, nt * nh - 1)

    nxt = lax.rem(t + 1, nt)
    prv = lax.rem(t + nt - 1, nt)
    up = pltpu.make_async_remote_copy(
        tail, halo.at[pl.ds(0, TAIL)], halo_s.at[0], halo_r.at[0], device_id=(nxt, h), device_id_type=MESH
    )
    down = pltpu.make_async_remote_copy(
        atoms_hbm.at[pl.ds(0, LEAD)],
        halo.at[pl.ds(TAIL, LEAD)],
        halo_s.at[1],
        halo_r.at[1],
        device_id=(prv, h),
        device_id_type=MESH,
    )
    pl.when(has_next)(up.start)
    pl.when(has_prev)(down.start)

    @pl.when(jnp.logical_not(has_prev))
    def _():
        halo[0:TAIL] = jnp.zeros((TAIL, halo.shape[1]), bf16)

    @pl.when(jnp.logical_not(has_next))
    def _():
        halo[TAIL:] = jnp.zeros((LEAD, halo.shape[1]), bf16)


    c_half = lax.rem(h, 2)
    locals_[3].wait()
    locals_[4].wait()
    sg[c_half, pl.ds(pl.multiple_of(t * rows, rows), rows), :] = single[
        :, pl.ds(pl.multiple_of(c_half * half, 128), half)
    ]
    wt[h] = w_tok[...]

    def head_send(src_of, dst, s, r):
        for peer in head_peers[1:]:
            pltpu.make_async_remote_copy(
                src_of(peer), dst.at[h], s, r, device_id=(t, peer), device_id_type=MESH
            ).start()

    def head_wait(ref, sem):
        total_wait(ref.at[pl.ds(0, nh - 1)], sem)

    own_rows = pl.ds(pl.multiple_of(t * rows, rows), rows)

    def start_sg(o, c):
        block = sg.at[c_half, own_rows, :]
        pltpu.make_async_remote_copy(
            block, block, sg_s, sg_r, device_id=(lax.rem(t + o, nt), h), device_id_type=MESH
        ).start()
        return c

    head_send(lambda peer: wt.at[h], wt, wt_s, wt_r)

    ri = iota((rows, rows), 0)
    ci = iota((rows, rows), 1)
    cnt_b = jnp.broadcast_to(cnt_row, (rows, rows))
    cnt_col = jnp.sum(jnp.where(ri == ci, cnt_b, 0.0), axis=1, keepdims=True)
    end_col = jnp.sum(jnp.where(ci <= ri, cnt_b, 0.0), axis=1, keepdims=True)
    end_i = end_col.astype(jnp.int32)
    start_i = (end_col - cnt_col).astype(jnp.int32)
    last = (live - 1) // QWIN
    r0 = (last - (EDGE - 1)) * QWIN

    locals_[2].wait()
    queries[...] = dot_t(atoms[...], w_atom[0]).astype(bf16)
    for ref, i in ((keys, 1), (values, 2)):
        ref[TAIL : TAIL + slots, :awidth] = dot_t(atoms[...], w_atom[i]).astype(bf16)
        ref[0:TAIL, :awidth] = jnp.zeros((TAIL, awidth), bf16)
        ref[TAIL + slots :, :awidth] = jnp.zeros((LEAD, awidth), bf16)
    values[:, awidth:] = jnp.ones((values.shape[0], values.shape[1] - awidth), bf16)

    scale = awidth ** (-0.5)
    qrows = GROUP * QWIN
    krows = qrows + KWIN
    lane = iota((1, krows), 1)
    first = iota((qrows, krows), 0) // QWIN * QWIN
    lanes = iota((qrows, krows), 1)
    band = jnp.where((lanes >= first) & (lanes < first + KWIN), 0.0, masked_value)
    wide_lane = iota((qrows, KWIN), 1)
    for w in range(slots // qrows):
        a = w * qrows
        pos = lane + (a - TAIL)
        outside = jnp.where((pos >= 0) & (pos < live), 0.0, masked_value)
        s = dot_t(queries[a : a + qrows], keys[a : a + krows, :]) * scale + (band + outside)
        top = jnp.max(s, axis=-1, keepdims=True)
        e = jnp.exp(s - top).astype(bf16)
        pv = dot(e, values[a : a + krows, :])
        inner[a : a + qrows] = jnp.where(wide_lane < 2 * awidth, pv, top)
        mixed[a : a + qrows] = (pv[:, :awidth] / pv[:, awidth : awidth + 1]).astype(bf16)

    lax.fori_loop(1, nt, start_sg, 0)
    slot = iota((rows, slots), 1)
    member = (slot >= start_i) & (slot < end_i)
    inside = member & (slot >= FRONT) & ((slot < r0) | (slot >= r0 + EDGE * QWIN))
    sums = dot(inside.astype(bf16), mixed[...])
    erow = iota((rows, FRONT + EDGE * QWIN), 1)
    eslot = jnp.where(erow < FRONT, erow, erow - FRONT + r0)
    touched = (eslot >= start_i) & (eslot < end_i) & ((erow < FRONT) | (eslot >= FRONT))
    touched = touched.astype(bf16)

    nrow = FRONT + EDGE * QWIN
    qi = iota((nrow, KWIN), 0)
    ki = iota((nrow, KWIN), 1)
    seen_prev = (qi < FRONT) & (ki < TAIL) & (ki >= qi // QWIN * QWIN) & has_prev
    reach = (qi - FRONT) // QWIN * QWIN + r0 + LEAD - live
    seen_next = (qi >= FRONT) & (ki >= TAIL) & (ki - TAIL < reach) & has_next
    edge_mask = jnp.where(seen_prev | seen_next, 0.0, masked_value)
    pick = iota((EDGE * QWIN, slots), 1) == iota((EDGE * QWIN, slots), 0) + r0
    a_edge = dot(pick.astype(bf16), atoms[...]).astype(bf16)
    a_edge = jnp.concatenate([atoms[0:FRONT], a_edge], axis=0)
    q_edge = dot_t(a_edge, w_atom[0]).astype(bf16)
    q_edge = dot(q_edge, w_atom[1]).astype(bf16)
    in_edge = jnp.dot(pick.astype(f32), inner[...], precision=lax.Precision.HIGHEST, preferred_element_type=f32)
    in_edge = jnp.concatenate([inner[0:FRONT], in_edge], axis=0)
    top_in = in_edge[:, 2 * awidth : 2 * awidth + 1]

    pl.when(has_prev)(up.wait_recv)
    pl.when(has_next)(down.wait_recv)
    vh = dot_t(halo[...], w_atom[2]).astype(bf16)
    vh = jnp.concatenate([vh, jnp.ones((KWIN, KWIN - awidth), bf16)], axis=1)
    s = dot_t(q_edge, halo[...]) * scale + edge_mask
    top_out = jnp.max(s, axis=-1, keepdims=True)
    e = jnp.exp(s - top_out).astype(bf16)
    pv = dot(e, vh)
    top = jnp.maximum(top_in, top_out)
    pv = jnp.exp(top_in - top) * in_edge + jnp.exp(top_out - top) * pv
    edge = (pv[:, :awidth] / pv[:, awidth : awidth + 1]).astype(bf16)
    means = (sums + dot(touched, edge)) / cnt_col
    packs = KWIN // awidth
    prow = rows // packs
    packed = jnp.concatenate([means[i * prow : (i + 1) * prow] for i in range(packs)], axis=1)
    ta[h, t] = packed.astype(bf16)

    def ta_send(pt, ph):
        block = ta.at[h, t]
        pltpu.make_async_remote_copy(
            block, block, ta_s, ta_r, device_id=(pt, ph), device_id_type=MESH
        ).start()

    everyone(ta_send, 1)

    locals_[5].wait()
    locals_[6].wait()
    for i in range(rows):
        pair_f[:, i, :] = dot_t(w_pair[...], pair[i])
    for p in range(nh):
        pair_s[p] = pair_f[p * local_heads : (p + 1) * local_heads].astype(bf16)
    pair_r[h] = pair_s[h]
    head_send(lambda peer: pair_s.at[peer], pair_r, pb_s, pb_r)

    locals_[7].wait()
    woven = w_raw[...].reshape(2 * width, hidden_width)
    blk = 128
    si = iota((blk, 2 * blk), 0)
    sj = iota((blk, 2 * blk), 1)
    picks = [(sj == 2 * si + p).astype(bf16) for p in (0, 1)]
    for b in range(width // blk):
        for p, ref in enumerate((w_gate, w_up)):
            ref[b * blk : (b + 1) * blk] = dot(picks[p], woven[2 * b * blk : 2 * (b + 1) * blk]).astype(bf16)

    at_window = iota((QWIN, awidth), 0) // QWIN
    for w in range(slots // QWIN):
        a = w * QWIN
        if a < FRONT:
            mixed[a : a + QWIN] = edge[a : a + QWIN]
        else:
            block = mixed[a : a + QWIN].astype(f32)
            for i in range(EDGE):
                b = FRONT + i * QWIN
                here = at_window + (w + EDGE - 1 - i) == last
                block = jnp.where(here, edge[b : b + QWIN].astype(f32), block)
            mixed[a : a + QWIN] = block.astype(bf16)
    alive = iota((slots, 1), 0) < live
    mix = jnp.where(alive, mixed[...].astype(f32), 0.0).astype(bf16)
    atom_mix[...] = dot_t(eye(awidth), mix).astype(bf16)

    total_wait(sg.at[0, pl.ds(0, (nt - 1) * rows), :], sg_r)
    partner = h + 1 - 2 * c_half
    fwd = pltpu.make_async_remote_copy(
        sg.at[c_half], sg.at[c_half], fwd_s, fwd_r, device_id=(t, partner), device_id_type=MESH
    )
    fwd.start()
    head_wait(wt, wt_r)
    head_wait(pair_r, pb_r)
    for i in range(8, 13):
        locals_[i].wait()
    fwd.wait_recv()
    flat_ta = ta.reshape(nh * nt, prow, packs * awidth).at[pl.ds(0, nh * nt - 1)]
    total_wait(flat_ta, ta_r)

    own = single[...].astype(f32)
    full = jnp.concatenate([sg[0], sg[1]], axis=1).astype(f32)
    at_lane = iota((1, packs * awidth), 1)

    def spread(x):
        x = x.astype(f32)
        return [
            jnp.where((at_lane >= i * awidth) & (at_lane < (i + 1) * awidth), x, 0.0)
            for i in range(packs)
        ]

    lhs = jnp.concatenate(
        [
            jnp.concatenate([m.reshape(nt, 1, prow, packs * awidth) for m in spread(ta[p].astype(f32).reshape(nt * prow, packs * awidth))], axis=1)
            .reshape(nt * rows, packs * awidth)
            .astype(bf16)
            for p in range(nh)
        ],
        axis=1,
    )
    own_lhs = jnp.concatenate(
        [jnp.concatenate(spread(ta[p, t]), axis=0).astype(bf16) for p in range(nh)], axis=1
    )
    wide = jnp.concatenate([wt[p] for p in range(nh) for i in range(packs)], axis=0)
    term = dot(lhs, wide)
    own_term = dot(own_lhs, wide)
    state = own + own_term
    normed_own = layer_norm(state, gain1[...].reshape(1, width)).astype(bf16)
    normed = layer_norm(full + term, gain1[...].reshape(1, width)).astype(bf16)
    q = dot_t(normed_own, w_proj[0])
    k = dot_t(normed, w_proj[1]).astype(bf16)
    v = dot_t(normed, w_proj[2]).astype(bf16)
    gate = jax.nn.sigmoid(dot_t(normed_own, w_proj[3]))
    col = iota((1, lw), 1)
    in_head = [(col >= hd * i) & (col < hd * (i + 1)) for i in range(local_heads)]
    stacked = jnp.concatenate([jnp.where(m, q, 0.0) for m in in_head], axis=0).astype(bf16)
    s = dot_t(stacked, k) * hd ** (-0.5)
    bias = jnp.concatenate(
        [pair_r[p].astype(f32).reshape(local_heads * rows, kblock) for p in range(nh)], axis=1
    )
    s = s + bias
    e = jnp.exp(s - jnp.max(s, axis=-1, keepdims=True))
    p_ = (e / jnp.sum(e, axis=-1, keepdims=True)).astype(bf16)
    ctx = dot(p_, v)
    context = jnp.zeros((rows, lw), f32)
    for i, m in enumerate(in_head):
        context = jnp.where(m, ctx[i * rows : (i + 1) * rows], context)
    gated = (context * gate).astype(bf16)
    parts[h] = dot(gated, w_out[...]).astype(bf16)
    head_send(lambda peer: parts.at[h], parts, part_s, part_r)

    pl.when(has_next)(up.wait_send)
    pl.when(has_prev)(down.wait_send)
    fwd.wait_send()
    head_wait(wt, wt_s)
    head_wait(pair_r, pb_s)
    total_wait(sg.at[0, pl.ds(0, (nt - 1) * rows), :], sg_s)
    total_wait(flat_ta, ta_s)

    head_wait(parts, part_r)
    total = parts[0].astype(f32)
    for p in range(1, nh):
        total += parts[p].astype(f32)
    after = state + total
    normed_after = layer_norm(after, gain2[...].reshape(1, width)).astype(bf16)
    g = dot(normed_after, w_gate[...])
    u = dot(normed_after, w_up[...])
    hidden = (jax.nn.silu(g) * u).astype(bf16)
    update = dot(hidden, w_down[...])
    quarter = width // nh
    for p in range(nh):
        fin_s_buf[p] = update[:, p * quarter : (p + 1) * quarter].astype(bf16)
    head_send(lambda peer: fin_s_buf.at[peer], fin_r_buf, fin_s, fin_r)
    for p in range(nh):
        own_buf[p] = after[:, p * quarter : (p + 1) * quarter]
    acc = own_buf[h] + fin_s_buf[h].astype(f32)
    fin_r_buf[h] = jnp.zeros((rows, quarter), bf16)
    head_wait(parts, part_s)
    head_wait(fin_r_buf, fin_s)
    head_wait(fin_r_buf, fin_r)
    for p in range(nh):
        acc += fin_r_buf[p].astype(f32)
    refined[...] = acc.astype(bf16)


def deliver(refined_in, mix_in, refined, atom_mix, sem):
    copies = [
        pltpu.make_async_copy(refined_in, refined, sem.at[0]),
        pltpu.make_async_copy(mix_in, atom_mix, sem.at[1]),
    ]
    for copy in copies:
        copy.start()
    for copy in copies:
        copy.wait()


def shards(
    nt,
    nh,
    single,
    pair,
    atoms,
    atom_counts,
    w_atom,
    w_atom_token,
    ln_gain,
    w_proj,
    w_pair_bias,
    w_out,
    ln_gain2,
    w_trans,
    w_trans_out,
):
    rows, width = single.shape
    slots, channels = atoms.shape
    awidth = w_atom.shape[2]
    heads = w_pair_bias.shape[1]
    local_heads = heads // nh
    kblock = pair.shape[1]
    n = nt * nh
    lw = w_proj.shape[2]
    hidden = w_trans.shape[2]
    quarter = width // nh
    vm = pl.BlockSpec(memory_space=pltpu.VMEM)
    hbm = pl.BlockSpec(memory_space=pltpu.HBM)
    dma = pltpu.SemaphoreType.DMA
    vmem = pltpu.VMEM
    refined, atom_mix = pl.pallas_call(
        functools.partial(kernel, nt, nh),
        out_shape=(vmem((rows, quarter), bf16), vmem((awidth, slots), bf16)),
        in_specs=[hbm] * 13,
        out_specs=(vm, vm),
        scratch_shapes=[
            vmem((1, rows), jnp.int32),
            vmem(single.shape, bf16),
            vmem(atoms.shape, bf16),
            vmem((3, awidth, channels), bf16),
            vmem(w_atom_token.shape, bf16),
            vmem(ln_gain.shape, bf16),
            vmem(ln_gain2.shape, bf16),
            vmem((heads, pair.shape[2]), bf16),
            vmem(pair.shape, bf16),
            vmem((4, lw, width), bf16),
            vmem(w_out.shape, bf16),
            vmem(w_trans.shape, bf16),
            vmem((width, hidden), bf16),
            vmem((width, hidden), bf16),
            vmem(w_trans_out.shape, bf16),
            dma((13,)),
            vmem((TAIL, channels), bf16),
            vmem((KWIN, channels), bf16),
            dma((2,)),
            dma((2,)),
            vmem((2, nt * rows, width // 2), bf16),
            dma,
            dma,
            dma,
            dma,
            vmem((nh, awidth, width), bf16),
            dma,
            dma,
            vmem((heads, rows, kblock), f32),
            vmem((nh, local_heads, rows, kblock), bf16),
            vmem((nh, local_heads, rows, kblock), bf16),
            dma,
            dma,
            vmem((slots, awidth), bf16),
            vmem((TAIL + slots + LEAD, awidth), bf16),
            vmem((TAIL + slots + LEAD, KWIN), bf16),
            vmem((slots, KWIN), f32),
            vmem((slots, awidth), bf16),
            vmem((nh, nt, rows * awidth // KWIN, KWIN), bf16),
            dma,
            dma,
            vmem((nh, rows, width), bf16),
            dma,
            dma,
            vmem((nh, rows, quarter), bf16),
            vmem((nh, rows, quarter), bf16),
            vmem((nh, rows, quarter), f32),
            dma,
            dma,
        ],
        compiler_params=pltpu.CompilerParams(
            collective_id=0, has_side_effects=True, vmem_limit_bytes=VMEM_MIB * 1024 * 1024
        ),
        name="step",
    )(
        single,
        pair,
        atoms,
        atom_counts.reshape(1, rows),
        jnp.transpose(w_atom, (1, 2, 0)),
        w_atom_token,
        ln_gain,
        jnp.transpose(w_proj, (1, 2, 0)),
        w_pair_bias.T,
        w_out,
        ln_gain2,
        w_trans,
        w_trans_out,
    )
    return pl.pallas_call(
        deliver,
        out_shape=(
            jax.ShapeDtypeStruct((rows, quarter), bf16),
            jax.ShapeDtypeStruct((awidth, slots), bf16),
        ),
        in_specs=[vm, vm],
        out_specs=(hbm, hbm),
        scratch_shapes=[dma((2,))],
        name="deliver",
    )(
        pltpu.with_memory_space_constraint(refined, pltpu.VMEM),
        pltpu.with_memory_space_constraint(atom_mix, pltpu.VMEM),
    )


def solution(mesh):
    return jax.shard_map(
        functools.partial(shards, mesh.shape["tok"], mesh.shape["head"]),
        mesh=mesh,
        in_specs=(
            P("tok", None),
            P("tok", "head", None),
            P("tok", None),
            P("tok"),
            P(None, None, "head"),
            P("head", None),
            P(),
            P(None, None, "head"),
            P(),
            P("head", None),
            P(),
            P(None, None, "head"),
            P("head", None),
        ),
        out_specs=(P("tok", "head"), P("head", "tok")),
        check_vma=False,
    )
```

```python
import functools

import jax
import jax.numpy as jnp
from jax import lax
from jax.experimental import pallas as pl
from jax.experimental.pallas import tpu as pltpu
from jax.sharding import PartitionSpec as P

H = 16
AH = 4
QWIN = 32
KWIN = 128
TAIL = (KWIN - QWIN) // 2
LEAD = (KWIN + QWIN) // 2
MESH = pl.DeviceIdType.MESH
f32 = jnp.float32
bf16 = jnp.bfloat16

norm_eps = 1e-05
masked_value = -1000000000.0
GROUP = 4
FRONT = 2 * QWIN
EDGE = 3
FRONT = 2 * QWIN
EDGE = 3
FRONT = 2 * QWIN
EDGE = 3
FRONT = 2 * QWIN
EDGE = 3
FRONT = 2 * QWIN
EDGE = 3
VMEM_MIB = 58


def dot(a, b):
    return jnp.dot(a, b, preferred_element_type=f32)


def dot_t(a, b):
    return lax.dot_general(a, b, (((1,), (1,)), ((), ())), preferred_element_type=f32)


def iota(shape, dim):
    return lax.broadcasted_iota(jnp.int32, shape, dim)


def eye(n):
    return (iota((n, n), 0) == iota((n, n), 1)).astype(bf16)


def layer_norm(x, gain):
    average = jnp.mean(x, axis=-1, keepdims=True)
    centred = x - average
    spread = jnp.mean(centred * centred, axis=-1, keepdims=True)
    return centred * lax.rsqrt(spread + norm_eps) * gain.astype(f32)


def total_wait(ref, sem):
    pltpu.make_async_copy(ref, ref, sem).wait()


def total_wait(ref, sem):
    pltpu.make_async_copy(ref, ref, sem).wait()


def total_wait(ref, sem):
    pltpu.make_async_copy(ref, ref, sem).wait()


def total_wait(ref, sem):
    pltpu.make_async_copy(ref, ref, sem).wait()


def total_wait(ref, sem):
    pltpu.make_async_copy(ref, ref, sem).wait()


def kernel(
    nt,
    nh,
    single_hbm,
    pair_hbm,
    atoms_hbm,
    counts_hbm,
    w_atom_hbm,
    w_tok_hbm,
    gain1_hbm,
    w_proj_hbm,
    w_pair_hbm,
    w_out_hbm,
    gain2_hbm,
    w_trans_hbm,
    w_down_hbm,
    refined,
    atom_mix,
    counts,
    single,
    atoms,
    w_atom,
    w_tok,
    gain1,
    gain2,
    w_pair,
    pair,
    w_proj,
    w_out,
    w_raw,
    w_gate,
    w_up,
    w_down,
    local_sem,
    relay,
    tail,
    halo,
    halo_s,
    halo_r,
    sg,
    sg_s,
    sg_r,
    fwd_s,
    fwd_r,
    wt,
    wt_s,
    wt_r,
    pair_f,
    pair_s,
    pair_r,
    pb_s,
    pb_r,
    queries,
    keys,
    values,
    inner,
    mixed,
    ta,
    ta_s,
    ta_r,
    parts,
    part_s,
    part_r,
    fin_s_buf,
    fin_r_buf,
    own_buf,
    fin_s,
    fin_r,
):
    t = lax.axis_index("tok")
    h = lax.axis_index("head")
    rows, width = single.shape
    slots = atoms.shape[0]
    awidth = w_atom.shape[1]
    heads = w_pair.shape[0]
    local_heads = heads // nh
    lw = w_proj.shape[1]
    hd = lw // local_heads
    kblock = pair.shape[1]
    half = width // 2
    hidden_width = w_gate.shape[1]

    barrier = pltpu.get_barrier_semaphore()
    head_peers = [lax.rem(h + o, nh) for o in range(nh)]

    has_next = t < nt - 1
    has_prev = t > 0
    below = t >= 2
    above = t + 2 < nt
    mate = t + 1 - 2 * lax.rem(t, 2)
    cross = t + 2 * lax.rem(t, 2) - 1
    has_cross = (cross >= 0) & (cross < nt)
    upper = t + 4 >= nt
    middle = jnp.logical_not(upper) & below
    lower = jnp.logical_not(upper) & jnp.logical_not(below)

    def tell(sem, pt, ph):
        pl.semaphore_signal(sem, inc=1, device_id=(pt, ph), device_id_type=MESH)

    tell(barrier, mate, h)
    pl.when(has_cross)(lambda: tell(barrier, cross, h))
    pl.when(below)(lambda: tell(barrier, t - 2, h))
    pl.when(above)(lambda: tell(barrier, t + 2, h))
    for peer in head_peers[1:]:
        tell(barrier, t, peer)
        tell(barrier, mate, peer)

    def other(o):
        return o + (o - t + nt) // nt

    def everyone(act):
        def step(o, c):
            for peer in head_peers:
                act(other(o), peer)
            return c

        lax.fori_loop(0, nt - 1, step, 0)
        for peer in head_peers[1:]:
            act(t, peer)

    locals_ = [
        pltpu.make_async_copy(src, dst, local_sem.at[i])
        for i, (src, dst) in enumerate(
            [
                (atoms_hbm, atoms),
                (counts_hbm, counts),
                (w_atom_hbm, w_atom),
                (single_hbm, single),
                (w_tok_hbm, w_tok),
                (w_pair_hbm, w_pair),
                (pair_hbm, pair),
                (w_trans_hbm, w_raw),
                (w_proj_hbm, w_proj),
                (gain1_hbm, gain1),
                (w_out_hbm, w_out),
                (gain2_hbm, gain2),
                (w_down_hbm, w_down),
            ]
        )
    ]
    for copy in locals_:
        copy.start()

    locals_[1].wait()
    cnt_row = counts[...].astype(f32)
    live = jnp.sum(cnt_row, axis=1, keepdims=True).astype(jnp.int32)
    locals_[0].wait()

    @pl.when(has_next)
    def _():
        pick = iota((TAIL, slots), 1) == iota((TAIL, slots), 0) + (live - TAIL)
        tail[...] = dot(pick.astype(bf16), atoms[...]).astype(bf16)

    some_below = (t + nt - 2) // nt
    some_above = (2 * nt - 3 - t) // nt
    some_cross = ((t + nt - 1) // nt) * ((2 * nt - 2 - t) // nt)
    pl.semaphore_wait(barrier, 2 * nh - 1 + some_cross + some_below + some_above)

    nxt = lax.rem(t + 1, nt)
    prv = lax.rem(t + nt - 1, nt)
    up = pltpu.make_async_remote_copy(
        tail, halo.at[pl.ds(0, TAIL)], halo_s.at[0], halo_r.at[0], device_id=(nxt, h), device_id_type=MESH
    )
    down = pltpu.make_async_remote_copy(
        atoms_hbm.at[pl.ds(0, LEAD)],
        halo.at[pl.ds(TAIL, LEAD)],
        halo_s.at[1],
        halo_r.at[1],
        device_id=(prv, h),
        device_id_type=MESH,
    )
    pl.when(has_next)(up.start)
    pl.when(has_prev)(down.start)

    @pl.when(jnp.logical_not(has_prev))
    def _():
        halo[0:TAIL] = jnp.zeros((TAIL, halo.shape[1]), bf16)

    @pl.when(jnp.logical_not(has_next))
    def _():
        halo[TAIL:] = jnp.zeros((LEAD, halo.shape[1]), bf16)


    from_below, from_above = relay.at[0], relay.at[1]
    pl.when(jnp.logical_not(below) & above)(lambda: tell(from_below, t + 2, h))
    pl.when(jnp.logical_not(above) & below)(lambda: tell(from_above, t - 2, h))
    pl.when(below)(lambda: pl.semaphore_wait(from_below, 1))
    pl.when(below & above)(lambda: tell(from_below, t + 2, h))

    def hear_above():
        pl.semaphore_wait(from_above, 1)
        pl.when(below)(lambda: tell(from_above, t - 2, h))

    pl.when(upper & above)(hear_above)

    c_half = lax.rem(h, 2)
    locals_[3].wait()
    locals_[4].wait()
    sg[c_half, pl.ds(pl.multiple_of(t * rows, rows), rows), :] = single[
        :, pl.ds(pl.multiple_of(c_half * half, 128), half)
    ]
    wt[h] = w_tok[...]

    def head_send(src_of, dst, s, r):
        for peer in head_peers[1:]:
            pltpu.make_async_remote_copy(
                src_of(peer), dst.at[h], s, r, device_id=(t, peer), device_id_type=MESH
            ).start()

    def head_wait(ref, sem):
        total_wait(ref.at[pl.ds(0, nh - 1)], sem)

    own_rows = pl.ds(pl.multiple_of(t * rows, rows), rows)

    def start_sg(o, c):
        block = sg.at[c_half, own_rows, :]
        pltpu.make_async_remote_copy(
            block, block, sg_s, sg_r, device_id=(other(o), h), device_id_type=MESH
        ).start()
        return c

    def send_single():
        lax.fori_loop(0, nt - 1, start_sg, 0)

    head_send(lambda peer: wt.at[h], wt, wt_s, wt_r)
    pl.when(upper)(send_single)

    ri = iota((rows, rows), 0)
    ci = iota((rows, rows), 1)
    cnt_b = jnp.broadcast_to(cnt_row, (rows, rows))
    cnt_col = jnp.sum(jnp.where(ri == ci, cnt_b, 0.0), axis=1, keepdims=True)
    end_col = jnp.sum(jnp.where(ci <= ri, cnt_b, 0.0), axis=1, keepdims=True)
    end_i = end_col.astype(jnp.int32)
    start_i = (end_col - cnt_col).astype(jnp.int32)
    last = (live - 1) // QWIN
    r0 = (last - (EDGE - 1)) * QWIN

    locals_[2].wait()
    queries[...] = dot_t(atoms[...], w_atom[0]).astype(bf16)
    for ref, i in ((keys, 1), (values, 2)):
        ref[TAIL : TAIL + slots, :awidth] = dot_t(atoms[...], w_atom[i]).astype(bf16)
        ref[0:TAIL, :awidth] = jnp.zeros((TAIL, awidth), bf16)
        ref[TAIL + slots :, :awidth] = jnp.zeros((LEAD, awidth), bf16)
    values[:, awidth:] = jnp.ones((values.shape[0], values.shape[1] - awidth), bf16)

    scale = awidth ** (-0.5)
    qrows = GROUP * QWIN
    krows = qrows + KWIN
    lane = iota((1, krows), 1)
    first = iota((qrows, krows), 0) // QWIN * QWIN
    lanes = iota((qrows, krows), 1)
    band = jnp.where((lanes >= first) & (lanes < first + KWIN), 0.0, masked_value)
    wide_lane = iota((qrows, KWIN), 1)
    for w in range(slots // qrows):
        a = w * qrows
        pos = lane + (a - TAIL)
        outside = jnp.where((pos >= 0) & (pos < live), 0.0, masked_value)
        s = dot_t(queries[a : a + qrows], keys[a : a + krows, :]) * scale + (band + outside)
        top = jnp.max(s, axis=-1, keepdims=True)
        e = jnp.exp(s - top).astype(bf16)
        pv = dot(e, values[a : a + krows, :])
        inner[a : a + qrows] = jnp.where(wide_lane < 2 * awidth, pv, top)
        mixed[a : a + qrows] = (pv[:, :awidth] / pv[:, awidth : awidth + 1]).astype(bf16)

    slot = iota((rows, slots), 1)
    member = (slot >= start_i) & (slot < end_i)
    inside = member & (slot >= FRONT) & ((slot < r0) | (slot >= r0 + EDGE * QWIN))
    sums = dot(inside.astype(bf16), mixed[...])
    erow = iota((rows, FRONT + EDGE * QWIN), 1)
    eslot = jnp.where(erow < FRONT, erow, erow - FRONT + r0)
    touched = (eslot >= start_i) & (eslot < end_i) & ((erow < FRONT) | (eslot >= FRONT))
    touched = touched.astype(bf16)

    nrow = FRONT + EDGE * QWIN
    qi = iota((nrow, KWIN), 0)
    ki = iota((nrow, KWIN), 1)
    seen_prev = (qi < FRONT) & (ki < TAIL) & (ki >= qi // QWIN * QWIN) & has_prev
    reach = (qi - FRONT) // QWIN * QWIN + r0 + LEAD - live
    seen_next = (qi >= FRONT) & (ki >= TAIL) & (ki - TAIL < reach) & has_next
    edge_mask = jnp.where(seen_prev | seen_next, 0.0, masked_value)
    pick = iota((EDGE * QWIN, slots), 1) == iota((EDGE * QWIN, slots), 0) + r0
    a_edge = dot(pick.astype(bf16), atoms[...]).astype(bf16)
    a_edge = jnp.concatenate([atoms[0:FRONT], a_edge], axis=0)
    q_edge = dot_t(a_edge, w_atom[0]).astype(bf16)
    q_edge = dot(q_edge, w_atom[1]).astype(bf16)
    in_edge = jnp.dot(pick.astype(f32), inner[...], precision=lax.Precision.HIGHEST, preferred_element_type=f32)
    in_edge = jnp.concatenate([inner[0:FRONT], in_edge], axis=0)
    top_in = in_edge[:, 2 * awidth : 2 * awidth + 1]

    pl.when(middle)(hear_above)
    pl.when(middle)(send_single)
    pl.when(has_prev)(up.wait_recv)
    pl.when(has_next)(down.wait_recv)
    vh = dot_t(halo[...], w_atom[2]).astype(bf16)
    vh = jnp.concatenate([vh, jnp.ones((KWIN, KWIN - awidth), bf16)], axis=1)
    s = dot_t(q_edge, halo[...]) * scale + edge_mask
    top_out = jnp.max(s, axis=-1, keepdims=True)
    e = jnp.exp(s - top_out).astype(bf16)
    pv = dot(e, vh)
    top = jnp.maximum(top_in, top_out)
    pv = jnp.exp(top_in - top) * in_edge + jnp.exp(top_out - top) * pv
    edge = (pv[:, :awidth] / pv[:, awidth : awidth + 1]).astype(bf16)
    means = (sums + dot(touched, edge)) / cnt_col
    packs = KWIN // awidth
    prow = rows // packs
    packed = jnp.concatenate([means[i * prow : (i + 1) * prow] for i in range(packs)], axis=1)
    ta[h, t] = packed.astype(bf16)

    def ta_send(pt, ph):
        block = ta.at[h, t]
        pltpu.make_async_remote_copy(
            block, block, ta_s, ta_r, device_id=(pt, ph), device_id_type=MESH
        ).start()

    pl.when(lower)(hear_above)
    everyone(ta_send)
    pl.when(lower)(send_single)

    locals_[5].wait()
    locals_[6].wait()
    for i in range(rows):
        pair_f[:, i, :] = dot_t(w_pair[...], pair[i])
    for p in range(nh):
        pair_s[p] = pair_f[p * local_heads : (p + 1) * local_heads].astype(bf16)
    pair_r[h] = pair_s[h]
    head_send(lambda peer: pair_s.at[peer], pair_r, pb_s, pb_r)

    locals_[7].wait()
    woven = w_raw[...].reshape(2 * width, hidden_width)
    blk = 128
    si = iota((blk, 2 * blk), 0)
    sj = iota((blk, 2 * blk), 1)
    picks = [(sj == 2 * si + p).astype(bf16) for p in (0, 1)]
    for b in range(width // blk):
        for p, ref in enumerate((w_gate, w_up)):
            ref[b * blk : (b + 1) * blk] = dot(picks[p], woven[2 * b * blk : 2 * (b + 1) * blk]).astype(bf16)

    at_window = iota((QWIN, awidth), 0) // QWIN
    for w in range(slots // QWIN):
        a = w * QWIN
        if a < FRONT:
            mixed[a : a + QWIN] = edge[a : a + QWIN]
        else:
            block = mixed[a : a + QWIN].astype(f32)
            for i in range(EDGE):
                b = FRONT + i * QWIN
                here = at_window + (w + EDGE - 1 - i) == last
                block = jnp.where(here, edge[b : b + QWIN].astype(f32), block)
            mixed[a : a + QWIN] = block.astype(bf16)
    alive = iota((slots, 1), 0) < live
    mix = jnp.where(alive, mixed[...].astype(f32), 0.0).astype(bf16)
    atom_mix[...] = dot_t(eye(awidth), mix).astype(bf16)

    total_wait(sg.at[0, pl.ds(0, (nt - 1) * rows), :], sg_r)
    partner = h + 1 - 2 * c_half
    fwd = pltpu.make_async_remote_copy(
        sg.at[c_half], sg.at[c_half], fwd_s, fwd_r, device_id=(t, partner), device_id_type=MESH
    )
    fwd.start()
    head_wait(wt, wt_r)
    head_wait(pair_r, pb_r)
    for i in range(8, 13):
        locals_[i].wait()
    fwd.wait_recv()
    flat_ta = ta.reshape(nh * nt, prow, packs * awidth).at[pl.ds(0, nh * nt - 1)]
    total_wait(flat_ta, ta_r)

    own = single[...].astype(f32)
    full = jnp.concatenate([sg[0], sg[1]], axis=1).astype(f32)
    at_lane = iota((1, packs * awidth), 1)

    def spread(x):
        x = x.astype(f32)
        return [
            jnp.where((at_lane >= i * awidth) & (at_lane < (i + 1) * awidth), x, 0.0)
            for i in range(packs)
        ]

    lhs = jnp.concatenate(
        [
            jnp.concatenate([m.reshape(nt, 1, prow, packs * awidth) for m in spread(ta[p].astype(f32).reshape(nt * prow, packs * awidth))], axis=1)
            .reshape(nt * rows, packs * awidth)
            .astype(bf16)
            for p in range(nh)
        ],
        axis=1,
    )
    own_lhs = jnp.concatenate(
        [jnp.concatenate(spread(ta[p, t]), axis=0).astype(bf16) for p in range(nh)], axis=1
    )
    wide = jnp.concatenate([wt[p] for p in range(nh) for i in range(packs)], axis=0)
    term = dot(lhs, wide)
    own_term = dot(own_lhs, wide)
    state = own + own_term
    normed_own = layer_norm(state, gain1[...].reshape(1, width)).astype(bf16)
    normed = layer_norm(full + term, gain1[...].reshape(1, width)).astype(bf16)
    q = dot_t(normed_own, w_proj[0])
    k = dot_t(normed, w_proj[1]).astype(bf16)
    v = dot_t(normed, w_proj[2]).astype(bf16)
    gate = jax.nn.sigmoid(dot_t(normed_own, w_proj[3]))
    col = iota((1, lw), 1)
    in_head = [(col >= hd * i) & (col < hd * (i + 1)) for i in range(local_heads)]
    stacked = jnp.concatenate([jnp.where(m, q, 0.0) for m in in_head], axis=0).astype(bf16)
    s = dot_t(stacked, k) * hd ** (-0.5)
    bias = jnp.concatenate(
        [pair_r[p].astype(f32).reshape(local_heads * rows, kblock) for p in range(nh)], axis=1
    )
    s = s + bias
    e = jnp.exp(s - jnp.max(s, axis=-1, keepdims=True))
    p_ = (e / jnp.sum(e, axis=-1, keepdims=True)).astype(bf16)
    ctx = dot(p_, v)
    context = jnp.zeros((rows, lw), f32)
    for i, m in enumerate(in_head):
        context = jnp.where(m, ctx[i * rows : (i + 1) * rows], context)
    gated = (context * gate).astype(bf16)
    parts[h] = dot(gated, w_out[...]).astype(bf16)
    head_send(lambda peer: parts.at[h], parts, part_s, part_r)

    pl.when(has_next)(up.wait_send)
    pl.when(has_prev)(down.wait_send)
    fwd.wait_send()
    head_wait(wt, wt_s)
    head_wait(pair_r, pb_s)
    total_wait(sg.at[0, pl.ds(0, (nt - 1) * rows), :], sg_s)
    total_wait(flat_ta, ta_s)

    head_wait(parts, part_r)
    total = parts[0].astype(f32)
    for p in range(1, nh):
        total += parts[p].astype(f32)
    after = state + total
    normed_after = layer_norm(after, gain2[...].reshape(1, width)).astype(bf16)
    g = dot(normed_after, w_gate[...])
    u = dot(normed_after, w_up[...])
    hidden = (jax.nn.silu(g) * u).astype(bf16)
    update = dot(hidden, w_down[...])
    quarter = width // nh
    for p in range(nh):
        fin_s_buf[p] = update[:, p * quarter : (p + 1) * quarter].astype(bf16)
    head_send(lambda peer: fin_s_buf.at[peer], fin_r_buf, fin_s, fin_r)
    for p in range(nh):
        own_buf[p] = after[:, p * quarter : (p + 1) * quarter]
    acc = own_buf[h] + fin_s_buf[h].astype(f32)
    fin_r_buf[h] = jnp.zeros((rows, quarter), bf16)
    head_wait(parts, part_s)
    head_wait(fin_r_buf, fin_s)
    head_wait(fin_r_buf, fin_r)
    for p in range(nh):
        acc += fin_r_buf[p].astype(f32)
    refined[...] = acc.astype(bf16)


def deliver(refined_in, mix_in, refined, atom_mix, sem):
    copies = [
        pltpu.make_async_copy(refined_in, refined, sem.at[0]),
        pltpu.make_async_copy(mix_in, atom_mix, sem.at[1]),
    ]
    for copy in copies:
        copy.start()
    for copy in copies:
        copy.wait()


def shards(
    nt,
    nh,
    single,
    pair,
    atoms,
    atom_counts,
    w_atom,
    w_atom_token,
    ln_gain,
    w_proj,
    w_pair_bias,
    w_out,
    ln_gain2,
    w_trans,
    w_trans_out,
):
    rows, width = single.shape
    slots, channels = atoms.shape
    awidth = w_atom.shape[2]
    heads = w_pair_bias.shape[1]
    local_heads = heads // nh
    kblock = pair.shape[1]
    n = nt * nh
    lw = w_proj.shape[2]
    hidden = w_trans.shape[2]
    quarter = width // nh
    vm = pl.BlockSpec(memory_space=pltpu.VMEM)
    hbm = pl.BlockSpec(memory_space=pltpu.HBM)
    dma = pltpu.SemaphoreType.DMA
    vmem = pltpu.VMEM
    refined, atom_mix = pl.pallas_call(
        functools.partial(kernel, nt, nh),
        out_shape=(vmem((rows, quarter), bf16), vmem((awidth, slots), bf16)),
        in_specs=[hbm] * 13,
        out_specs=(vm, vm),
        scratch_shapes=[
            vmem((1, rows), jnp.int32),
            vmem(single.shape, bf16),
            vmem(atoms.shape, bf16),
            vmem((3, awidth, channels), bf16),
            vmem(w_atom_token.shape, bf16),
            vmem(ln_gain.shape, bf16),
            vmem(ln_gain2.shape, bf16),
            vmem((heads, pair.shape[2]), bf16),
            vmem(pair.shape, bf16),
            vmem((4, lw, width), bf16),
            vmem(w_out.shape, bf16),
            vmem(w_trans.shape, bf16),
            vmem((width, hidden), bf16),
            vmem((width, hidden), bf16),
            vmem(w_trans_out.shape, bf16),
            dma((13,)),
            pltpu.SemaphoreType.REGULAR((2,)),
            vmem((TAIL, channels), bf16),
            vmem((KWIN, channels), bf16),
            dma((2,)),
            dma((2,)),
            vmem((2, nt * rows, width // 2), bf16),
            dma,
            dma,
            dma,
            dma,
            vmem((nh, awidth, width), bf16),
            dma,
            dma,
            vmem((heads, rows, kblock), f32),
            vmem((nh, local_heads, rows, kblock), bf16),
            vmem((nh, local_heads, rows, kblock), bf16),
            dma,
            dma,
            vmem((slots, awidth), bf16),
            vmem((TAIL + slots + LEAD, awidth), bf16),
            vmem((TAIL + slots + LEAD, KWIN), bf16),
            vmem((slots, KWIN), f32),
            vmem((slots, awidth), bf16),
            vmem((nh, nt, rows * awidth // KWIN, KWIN), bf16),
            dma,
            dma,
            vmem((nh, rows, width), bf16),
            dma,
            dma,
            vmem((nh, rows, quarter), bf16),
            vmem((nh, rows, quarter), bf16),
            vmem((nh, rows, quarter), f32),
            dma,
            dma,
        ],
        compiler_params=pltpu.CompilerParams(
            collective_id=0, has_side_effects=True, vmem_limit_bytes=VMEM_MIB * 1024 * 1024
        ),
        name="step",
    )(
        single,
        pair,
        atoms,
        atom_counts.reshape(1, rows),
        jnp.transpose(w_atom, (1, 2, 0)),
        w_atom_token,
        ln_gain,
        jnp.transpose(w_proj, (1, 2, 0)),
        w_pair_bias.T,
        w_out,
        ln_gain2,
        w_trans,
        w_trans_out,
    )
    return pl.pallas_call(
        deliver,
        out_shape=(
            jax.ShapeDtypeStruct((rows, quarter), bf16),
            jax.ShapeDtypeStruct((awidth, slots), bf16),
        ),
        in_specs=[vm, vm],
        out_specs=(hbm, hbm),
        scratch_shapes=[dma((2,))],
        name="deliver",
    )(
        pltpu.with_memory_space_constraint(refined, pltpu.VMEM),
        pltpu.with_memory_space_constraint(atom_mix, pltpu.VMEM),
    )


def solution(mesh):
    return jax.shard_map(
        functools.partial(shards, mesh.shape["tok"], mesh.shape["head"]),
        mesh=mesh,
        in_specs=(
            P("tok", None),
            P("tok", "head", None),
            P("tok", None),
            P("tok"),
            P(None, None, "head"),
            P("head", None),
            P(),
            P(None, None, "head"),
            P(),
            P("head", None),
            P(),
            P(None, None, "head"),
            P("head", None),
        ),
        out_specs=(P("tok", "head"), P("head", "tok")),
        check_vma=False,
    )
```

```python
import functools

import jax
import jax.numpy as jnp
from jax import lax
from jax.experimental import pallas as pl
from jax.experimental.pallas import tpu as pltpu
from jax.sharding import PartitionSpec as P

H = 16
AH = 4
QWIN = 32
KWIN = 128
TAIL = (KWIN - QWIN) // 2
LEAD = (KWIN + QWIN) // 2
MESH = pl.DeviceIdType.MESH
f32 = jnp.float32
bf16 = jnp.bfloat16

norm_eps = 1e-05
masked_value = -1000000000.0
GROUP = 4
FRONT = 2 * QWIN
EDGE = 3
FRONT = 2 * QWIN
EDGE = 3
FRONT = 2 * QWIN
EDGE = 3
FRONT = 2 * QWIN
EDGE = 3
FRONT = 2 * QWIN
EDGE = 3
VMEM_MIB = 58


def dot(a, b):
    return jnp.dot(a, b, preferred_element_type=f32)


def dot_t(a, b):
    return lax.dot_general(a, b, (((1,), (1,)), ((), ())), preferred_element_type=f32)


def iota(shape, dim):
    return lax.broadcasted_iota(jnp.int32, shape, dim)


def eye(n):
    return (iota((n, n), 0) == iota((n, n), 1)).astype(bf16)


def layer_norm(x, gain):
    average = jnp.mean(x, axis=-1, keepdims=True)
    centred = x - average
    spread = jnp.mean(centred * centred, axis=-1, keepdims=True)
    return centred * lax.rsqrt(spread + norm_eps) * gain.astype(f32)


def total_wait(ref, sem):
    pltpu.make_async_copy(ref, ref, sem).wait()


def total_wait(ref, sem):
    pltpu.make_async_copy(ref, ref, sem).wait()


def total_wait(ref, sem):
    pltpu.make_async_copy(ref, ref, sem).wait()


def total_wait(ref, sem):
    pltpu.make_async_copy(ref, ref, sem).wait()


def total_wait(ref, sem):
    pltpu.make_async_copy(ref, ref, sem).wait()


def kernel(
    nt,
    nh,
    single_hbm,
    pair_hbm,
    atoms_hbm,
    counts_hbm,
    w_atom_hbm,
    w_tok_hbm,
    gain1_hbm,
    w_proj_hbm,
    w_pair_hbm,
    w_out_hbm,
    gain2_hbm,
    w_trans_hbm,
    w_down_hbm,
    refined,
    atom_mix,
    counts,
    single,
    atoms,
    w_atom,
    w_tok,
    gain1,
    gain2,
    w_pair,
    pair,
    w_proj,
    w_raw,
    w_gate,
    w_up,
    w_down,
    local_sem,
    relay,
    tail,
    halo,
    halo_s,
    halo_r,
    sg,
    sg_s,
    sg_r,
    fwd_s,
    fwd_r,
    wt,
    wt_s,
    wt_r,
    pair_f,
    pair_s,
    pair_r,
    pb_s,
    pb_r,
    queries,
    keys,
    values,
    inner,
    mixed,
    atoms_in,
    state_in,
    normed_all,
    bias,
    ta,
    ta_s,
    ta_r,
    wo,
    wo_s,
    wo_r,
    gat,
    gat_s,
    gat_r,
    fin_s_buf,
    fin_r_buf,
    own_buf,
    fin_s,
    fin_r,
):
    t = lax.axis_index("tok")
    h = lax.axis_index("head")
    rows, width = single.shape
    slots = atoms.shape[0]
    awidth = w_atom.shape[1]
    heads = w_pair.shape[0]
    local_heads = heads // nh
    lw = w_proj.shape[1]
    hd = lw // local_heads
    kblock = pair.shape[1]
    half = width // 2
    hidden_width = w_gate.shape[1]

    barrier = pltpu.get_barrier_semaphore()
    head_peers = [lax.rem(h + o, nh) for o in range(nh)]

    has_next = t < nt - 1
    has_prev = t > 0
    below = t >= 2
    above = t + 2 < nt
    mate = t + 1 - 2 * lax.rem(t, 2)
    cross = t + 2 * lax.rem(t, 2) - 1
    upper = t + 4 >= nt
    middle = jnp.logical_not(upper) & below
    lower = jnp.logical_not(upper) & jnp.logical_not(below)

    def tell(sem, pt, ph):
        pl.semaphore_signal(sem, inc=1, device_id=(pt, ph), device_id_type=MESH)

    tell(barrier, mate, h)
    pl.when(below & (cross < t))(lambda: tell(barrier, cross, h))
    pl.when(below)(lambda: tell(barrier, t - 2, h))
    for peer in head_peers[1:]:
        tell(barrier, t, peer)
        tell(barrier, mate, peer)

    def tell_later(o, c):
        for peer in head_peers:
            tell(barrier, o, peer)
        return c

    lax.fori_loop(2 * (t // 2) + 2, nt, tell_later, 0)

    def other(o):
        return o + (o - t + nt) // nt

    def everyone(act):
        def step(o, c):
            for peer in head_peers:
                act(other(o), peer)
            return c

        lax.fori_loop(0, nt - 1, step, 0)
        for peer in head_peers[1:]:
            act(t, peer)

    locals_ = [
        pltpu.make_async_copy(src, dst, local_sem.at[i])
        for i, (src, dst) in enumerate(
            [
                (atoms_hbm, atoms),
                (counts_hbm, counts),
                (w_atom_hbm, w_atom),
                (single_hbm, single),
                (w_tok_hbm, w_tok),
                (w_pair_hbm, w_pair),
                (pair_hbm, pair),
                (w_trans_hbm, w_raw),
                (w_proj_hbm, w_proj),
                (gain1_hbm, gain1),
                (w_out_hbm, wo.at[h]),
                (gain2_hbm, gain2),
                (w_down_hbm, w_down),
            ]
        )
    ]
    for copy in locals_:
        copy.start()

    locals_[1].wait()
    cnt_row = counts[...].astype(f32)
    live = jnp.sum(cnt_row, axis=1, keepdims=True).astype(jnp.int32)
    locals_[0].wait()

    @pl.when(has_next)
    def _():
        pick = iota((TAIL, slots), 1) == iota((TAIL, slots), 0) + (live - TAIL)
        tail[...] = dot(pick.astype(bf16), atoms[...]).astype(bf16)

    earlier = (t // 2) * 2 * nh
    some_above = (2 * nt - 3 - t) // nt
    some_cross = lax.rem(t, 2) * ((2 * nt - 2 - t) // nt)
    pl.semaphore_wait(barrier, earlier + 2 * nh - 1 + some_cross + some_above)

    nxt = lax.rem(t + 1, nt)
    prv = lax.rem(t + nt - 1, nt)
    up = pltpu.make_async_remote_copy(
        tail, halo.at[pl.ds(0, TAIL)], halo_s.at[0], halo_r.at[0], device_id=(nxt, h), device_id_type=MESH
    )
    down = pltpu.make_async_remote_copy(
        atoms_hbm.at[pl.ds(0, LEAD)],
        halo.at[pl.ds(TAIL, LEAD)],
        halo_s.at[1],
        halo_r.at[1],
        device_id=(prv, h),
        device_id_type=MESH,
    )
    pl.when(has_next)(up.start)
    pl.when(has_prev)(down.start)

    @pl.when(jnp.logical_not(has_prev))
    def _():
        halo[0:TAIL] = jnp.zeros((TAIL, halo.shape[1]), bf16)

    @pl.when(jnp.logical_not(has_next))
    def _():
        halo[TAIL:] = jnp.zeros((LEAD, halo.shape[1]), bf16)


    pl.when(jnp.logical_not(above) & below)(lambda: tell(relay, t - 2, h))

    def hear_above():
        pl.semaphore_wait(relay, 1)
        pl.when(below)(lambda: tell(relay, t - 2, h))

    c_half = lax.rem(h, 2)
    locals_[3].wait()
    locals_[4].wait()
    sg[c_half, pl.ds(pl.multiple_of(t * rows, rows), rows), :] = single[
        :, pl.ds(pl.multiple_of(c_half * half, 128), half)
    ]
    wt[h] = w_tok[...]

    def head_send(src_of, dst, s, r):
        for peer in head_peers[1:]:
            pltpu.make_async_remote_copy(
                src_of(peer), dst.at[h], s, r, device_id=(t, peer), device_id_type=MESH
            ).start()

    def head_wait(ref, sem):
        total_wait(ref.at[pl.ds(0, nh - 1)], sem)

    own_rows = pl.ds(pl.multiple_of(t * rows, rows), rows)

    def start_sg(o, c):
        block = sg.at[c_half, own_rows, :]
        pltpu.make_async_remote_copy(
            block, block, sg_s, sg_r, device_id=(other(o), h), device_id_type=MESH
        ).start()
        return c

    def send_single():
        lax.fori_loop(0, nt - 1, start_sg, 0)

    head_send(lambda peer: wt.at[h], wt, wt_s, wt_r)

    partner = h + 1 - 2 * c_half
    across = [lax.rem(h + o, nh) for o in range(2, nh, 2)]
    first_part = lw // 4 // 16 * 16

    def give(ref, peer, s, r):
        return pltpu.make_async_remote_copy(ref, ref, s, r, device_id=(t, peer), device_id_type=MESH)

    def give_rows(start, size):
        for peer in across:
            give(wo.at[h, pl.ds(start, size)], peer, wo_s.at[1], wo_r.at[1]).start()


    def give_first():
        locals_[10].wait()
        give_rows(0, first_part)

    pl.when(jnp.logical_not(upper))(give_first)
    pl.when(upper & jnp.logical_not(above))(send_single)

    ri = iota((rows, rows), 0)
    ci = iota((rows, rows), 1)
    cnt_b = jnp.broadcast_to(cnt_row, (rows, rows))
    cnt_col = jnp.sum(jnp.where(ri == ci, cnt_b, 0.0), axis=1, keepdims=True)
    end_col = jnp.sum(jnp.where(ci <= ri, cnt_b, 0.0), axis=1, keepdims=True)
    end_i = end_col.astype(jnp.int32)
    start_i = (end_col - cnt_col).astype(jnp.int32)
    last = (live - 1) // QWIN
    r0 = (last - (EDGE - 1)) * QWIN

    locals_[2].wait()
    queries[...] = dot_t(atoms[...], w_atom[0]).astype(bf16)
    for ref, i in ((keys, 1), (values, 2)):
        ref[TAIL : TAIL + slots, :awidth] = dot_t(atoms[...], w_atom[i]).astype(bf16)
        ref[0:TAIL, :awidth] = jnp.zeros((TAIL, awidth), bf16)
        ref[TAIL + slots :, :awidth] = jnp.zeros((LEAD, awidth), bf16)
    values[:, awidth:] = jnp.ones((values.shape[0], values.shape[1] - awidth), bf16)

    scale = awidth ** (-0.5)
    qrows = GROUP * QWIN
    krows = qrows + KWIN
    lane = iota((1, krows), 1)
    first = iota((qrows, krows), 0) // QWIN * QWIN
    lanes = iota((qrows, krows), 1)
    band = jnp.where((lanes >= first) & (lanes < first + KWIN), 0.0, masked_value)
    wide_lane = iota((qrows, KWIN), 1)
    for w in range(slots // qrows):
        a = w * qrows
        pos = lane + (a - TAIL)
        outside = jnp.where((pos >= 0) & (pos < live), 0.0, masked_value)
        s = dot_t(queries[a : a + qrows], keys[a : a + krows, :]) * scale + (band + outside)
        top = jnp.max(s, axis=-1, keepdims=True)
        e = jnp.exp(s - top).astype(bf16)
        pv = dot(e, values[a : a + krows, :])
        inner[a : a + qrows] = jnp.where(wide_lane < 2 * awidth, pv, top)
        mixed[a : a + qrows] = (pv[:, :awidth] / pv[:, awidth : awidth + 1]).astype(bf16)

    pl.when(upper & above)(hear_above)
    pl.when(upper & above)(send_single)
    slot = iota((rows, slots), 1)
    member = (slot >= start_i) & (slot < end_i)
    inside = member & (slot >= FRONT) & ((slot < r0) | (slot >= r0 + EDGE * QWIN))
    sums = dot(inside.astype(bf16), mixed[...])
    erow = iota((rows, FRONT + EDGE * QWIN), 1)
    eslot = jnp.where(erow < FRONT, erow, erow - FRONT + r0)
    touched = (eslot >= start_i) & (eslot < end_i) & ((erow < FRONT) | (eslot >= FRONT))
    touched = touched.astype(bf16)

    nrow = FRONT + EDGE * QWIN
    qi = iota((nrow, KWIN), 0)
    ki = iota((nrow, KWIN), 1)
    seen_prev = (qi < FRONT) & (ki < TAIL) & (ki >= qi // QWIN * QWIN) & has_prev
    reach = (qi - FRONT) // QWIN * QWIN + r0 + LEAD - live
    seen_next = (qi >= FRONT) & (ki >= TAIL) & (ki - TAIL < reach) & has_next
    edge_mask = jnp.where(seen_prev | seen_next, 0.0, masked_value)
    pick = iota((EDGE * QWIN, slots), 1) == iota((EDGE * QWIN, slots), 0) + r0
    a_edge = dot(pick.astype(bf16), atoms[...]).astype(bf16)
    a_edge = jnp.concatenate([atoms[0:FRONT], a_edge], axis=0)
    q_edge = dot_t(a_edge, w_atom[0]).astype(bf16)
    q_edge = dot(q_edge, w_atom[1]).astype(bf16)
    in_edge = jnp.dot(pick.astype(f32), inner[...], precision=lax.Precision.HIGHEST, preferred_element_type=f32)
    in_edge = jnp.concatenate([inner[0:FRONT], in_edge], axis=0)
    top_in = in_edge[:, 2 * awidth : 2 * awidth + 1]

    locals_[5].wait()
    locals_[6].wait()
    for i in range(rows):
        pair_f[:, i, :] = dot_t(w_pair[...], pair[i])
    for p in range(nh):
        pair_s[p] = pair_f[p * local_heads : (p + 1) * local_heads].astype(bf16)
    pair_r[h] = pair_s[h]
    head_send(lambda peer: pair_s.at[peer], pair_r, pb_s, pb_r)

    pl.when(middle)(hear_above)
    pl.when(middle)(send_single)
    pl.when(has_prev)(up.wait_recv)
    pl.when(has_next)(down.wait_recv)
    vh = dot_t(halo[...], w_atom[2]).astype(bf16)
    vh = jnp.concatenate([vh, jnp.ones((KWIN, KWIN - awidth), bf16)], axis=1)
    s = dot_t(q_edge, halo[...]) * scale + edge_mask
    top_out = jnp.max(s, axis=-1, keepdims=True)
    e = jnp.exp(s - top_out).astype(bf16)
    pv = dot(e, vh)
    top = jnp.maximum(top_in, top_out)
    pv = jnp.exp(top_in - top) * in_edge + jnp.exp(top_out - top) * pv
    edge = (pv[:, :awidth] / pv[:, awidth : awidth + 1]).astype(bf16)
    means = (sums + dot(touched, edge)) / cnt_col
    packs = KWIN // awidth
    prow = rows // packs
    packed = jnp.concatenate([means[i * prow : (i + 1) * prow] for i in range(packs)], axis=1)
    ta[h, t] = packed.astype(bf16)

    def ta_send(pt, ph):
        block = ta.at[h, t]
        pltpu.make_async_remote_copy(
            block, block, ta_s, ta_r, device_id=(pt, ph), device_id_type=MESH
        ).start()

    pl.when(lower)(hear_above)
    everyone(ta_send)
    pl.when(lower)(send_single)

    locals_[7].wait()
    woven = w_raw[...].reshape(2 * width, hidden_width)
    blk = 128
    si = iota((blk, 2 * blk), 0)
    sj = iota((blk, 2 * blk), 1)
    picks = [(sj == 2 * si + p).astype(bf16) for p in (0, 1)]
    for b in range(width // blk):
        for p, ref in enumerate((w_gate, w_up)):
            ref[b * blk : (b + 1) * blk] = dot(picks[p], woven[2 * b * blk : 2 * (b + 1) * blk]).astype(bf16)

    at_window = iota((QWIN, awidth), 0) // QWIN
    for w in range(slots // QWIN):
        a = w * QWIN
        if a < FRONT:
            mixed[a : a + QWIN] = edge[a : a + QWIN]
        else:
            block = mixed[a : a + QWIN].astype(f32)
            for i in range(EDGE):
                b = FRONT + i * QWIN
                here = at_window + (w + EDGE - 1 - i) == last
                block = jnp.where(here, edge[b : b + QWIN].astype(f32), block)
            mixed[a : a + QWIN] = block.astype(bf16)
    alive = iota((slots, 1), 0) < live
    mix = jnp.where(alive, mixed[...].astype(f32), 0.0).astype(bf16)
    atom_mix[...] = dot_t(eye(awidth), mix).astype(bf16)

    pl.when(upper)(give_first)
    give(wo.at[h], partner, wo_s.at[0], wo_r.at[0]).start()
    give_rows(first_part, lw - first_part)
    total_wait(sg.at[0, pl.ds(0, (nt - 1) * rows), :], sg_r)
    fwd = pltpu.make_async_remote_copy(
        sg.at[c_half], sg.at[c_half], fwd_s, fwd_r, device_id=(t, partner), device_id_type=MESH
    )
    fwd.start()
    head_wait(wt, wt_r)
    head_wait(pair_r, pb_r)
    for i in (8, 9, 11, 12):
        locals_[i].wait()
    bias[...] = jnp.concatenate(
        [pair_r[p].astype(f32).reshape(local_heads * rows, kblock) for p in range(nh)], axis=1
    )
    fwd.wait_recv()
    for i in range(2):
        state_in[:, i * half : (i + 1) * half] = sg[i].astype(f32)
    flat_ta = ta.reshape(nh * nt, prow, packs * awidth).at[pl.ds(0, nh * nt - 1)]
    total_wait(flat_ta, ta_r)

    at_lane = iota((1, packs * awidth), 1)
    blocks = [ta[p].astype(f32).reshape(nt * prow, packs * awidth) for p in range(nh)]
    turned = []
    for i in range(packs):
        block = blocks[0]
        for p in range(nh):
            moved = blocks[p]
            if p != i:
                moved = pltpu.roll(moved, (p - i) % packs * awidth, axis=1)
            block = moved if p == 0 else jnp.where(at_lane >= p * awidth, moved, block)
        turned.append(block.reshape(nt, 1, prow, packs * awidth))
    lhs = jnp.concatenate(turned, axis=1).reshape(nt * rows, packs * awidth).astype(bf16)
    atoms_in[...] = lhs
    w_full = wt[...].reshape(nh * awidth, width)
    normed_all[...] = layer_norm(state_in[...] + dot(lhs, w_full), gain1[...].reshape(1, width)).astype(bf16)
    normed_own = normed_all[own_rows, :]
    q = dot_t(normed_own, w_proj[0])
    k = dot_t(normed_all[...], w_proj[1]).astype(bf16)
    col = iota((1, lw), 1)
    in_head = [(col >= hd * i) & (col < hd * (i + 1)) for i in range(local_heads)]
    stacked = jnp.concatenate([jnp.where(m, q, 0.0) for m in in_head], axis=0).astype(bf16)
    s = dot_t(stacked, k) * hd ** (-0.5)
    v = dot_t(normed_all[...], w_proj[2]).astype(bf16)
    gate = jax.nn.sigmoid(dot_t(normed_own, w_proj[3]))
    s = s + bias[...]
    e = jnp.exp(s - jnp.max(s, axis=-1, keepdims=True))
    ctx = dot(e.astype(bf16), v) / jnp.sum(e, axis=-1, keepdims=True)
    context = jnp.zeros((rows, lw), f32)
    for i, m in enumerate(in_head):
        context = jnp.where(m, ctx[i * rows : (i + 1) * rows], context)
    gated = (context * gate).astype(bf16)
    gat[h] = gated
    for peer in across:
        for far in (peer, peer + 1 - 2 * c_half):
            give(gat.at[h], far, gat_s.at[1], gat_r.at[1]).start()
    give(gat.at[h], partner, gat_s.at[0], gat_r.at[0]).start()
    state = single[...].astype(f32) + dot(atoms_in[own_rows, :], wt[...].reshape(nh * awidth, width))
    n_across = len(across)
    total_wait(wo.at[pl.ds(0, n_across)], wo_r.at[1])
    for peer in across:
        give(wo.at[peer], partner, wo_s.at[2], wo_r.at[2]).start()
    after = state + dot(gated, wo[h])
    total_wait(wo.at[0], wo_r.at[0])
    total_wait(gat.at[0], gat_r.at[0])
    after += dot(gat[partner], wo[partner])

    pl.when(has_next)(up.wait_send)
    pl.when(has_prev)(down.wait_send)
    fwd.wait_send()
    head_wait(wt, wt_s)
    head_wait(pair_r, pb_s)
    total_wait(sg.at[0, pl.ds(0, (nt - 1) * rows), :], sg_s)
    total_wait(flat_ta, ta_s)

    total_wait(wo.at[0], wo_s.at[0])
    total_wait(wo.at[pl.ds(0, n_across)], wo_s.at[1])
    total_wait(wo.at[pl.ds(0, n_across)], wo_r.at[2])
    total_wait(gat.at[pl.ds(0, 2 * n_across)], gat_r.at[1])
    for peer in across:
        for far in (peer, peer + 1 - 2 * c_half):
            after += dot(gat[far], wo[far])
    normed_after = layer_norm(after, gain2[...].reshape(1, width)).astype(bf16)
    g = dot(normed_after, w_gate[...])
    u = dot(normed_after, w_up[...])
    hidden = (jax.nn.silu(g) * u).astype(bf16)
    update = dot(hidden, w_down[...])
    quarter = width // nh
    for p in range(nh):
        fin_s_buf[p] = update[:, p * quarter : (p + 1) * quarter].astype(bf16)
    head_send(lambda peer: fin_s_buf.at[peer], fin_r_buf, fin_s, fin_r)
    for p in range(nh):
        own_buf[p] = after[:, p * quarter : (p + 1) * quarter]
    acc = own_buf[h] + fin_s_buf[h].astype(f32)
    fin_r_buf[h] = jnp.zeros((rows, quarter), bf16)
    total_wait(gat.at[0], gat_s.at[0])
    total_wait(gat.at[pl.ds(0, 2 * n_across)], gat_s.at[1])
    total_wait(wo.at[pl.ds(0, n_across)], wo_s.at[2])
    head_wait(fin_r_buf, fin_s)
    head_wait(fin_r_buf, fin_r)
    for p in range(nh):
        acc += fin_r_buf[p].astype(f32)
    refined[...] = acc.astype(bf16)


def deliver(refined_in, mix_in, refined, atom_mix, sem):
    copies = [
        pltpu.make_async_copy(refined_in, refined, sem.at[0]),
        pltpu.make_async_copy(mix_in, atom_mix, sem.at[1]),
    ]
    for copy in copies:
        copy.start()
    for copy in copies:
        copy.wait()


def shards(
    nt,
    nh,
    single,
    pair,
    atoms,
    atom_counts,
    w_atom,
    w_atom_token,
    ln_gain,
    w_proj,
    w_pair_bias,
    w_out,
    ln_gain2,
    w_trans,
    w_trans_out,
):
    rows, width = single.shape
    slots, channels = atoms.shape
    awidth = w_atom.shape[2]
    heads = w_pair_bias.shape[1]
    local_heads = heads // nh
    kblock = pair.shape[1]
    n = nt * nh
    lw = w_proj.shape[2]
    hidden = w_trans.shape[2]
    quarter = width // nh
    vm = pl.BlockSpec(memory_space=pltpu.VMEM)
    hbm = pl.BlockSpec(memory_space=pltpu.HBM)
    dma = pltpu.SemaphoreType.DMA
    vmem = pltpu.VMEM
    refined, atom_mix = pl.pallas_call(
        functools.partial(kernel, nt, nh),
        out_shape=(vmem((rows, quarter), bf16), vmem((awidth, slots), bf16)),
        in_specs=[hbm] * 13,
        out_specs=(vm, vm),
        scratch_shapes=[
            vmem((1, rows), jnp.int32),
            vmem(single.shape, bf16),
            vmem(atoms.shape, bf16),
            vmem((3, awidth, channels), bf16),
            vmem(w_atom_token.shape, bf16),
            vmem(ln_gain.shape, bf16),
            vmem(ln_gain2.shape, bf16),
            vmem((heads, pair.shape[2]), bf16),
            vmem(pair.shape, bf16),
            vmem((4, lw, width), bf16),
            vmem(w_trans.shape, bf16),
            vmem((width, hidden), bf16),
            vmem((width, hidden), bf16),
            vmem(w_trans_out.shape, bf16),
            dma((13,)),
            pltpu.SemaphoreType.REGULAR,
            vmem((TAIL, channels), bf16),
            vmem((KWIN, channels), bf16),
            dma((2,)),
            dma((2,)),
            vmem((2, nt * rows, width // 2), bf16),
            dma,
            dma,
            dma,
            dma,
            vmem((nh, awidth, width), bf16),
            dma,
            dma,
            vmem((heads, rows, kblock), f32),
            vmem((nh, local_heads, rows, kblock), bf16),
            vmem((nh, local_heads, rows, kblock), bf16),
            dma,
            dma,
            vmem((slots, awidth), bf16),
            vmem((TAIL + slots + LEAD, awidth), bf16),
            vmem((TAIL + slots + LEAD, KWIN), bf16),
            vmem((slots, KWIN), f32),
            vmem((slots, awidth), bf16),
            vmem((nt * rows, nh * awidth), bf16),
            vmem((nt * rows, width), f32),
            vmem((nt * rows, width), bf16),
            vmem((local_heads * rows, nh * kblock), f32),
            vmem((nh, nt, rows * awidth // KWIN, KWIN), bf16),
            dma,
            dma,
            vmem((nh, lw, width), bf16),
            dma((3,)),
            dma((3,)),
            vmem((nh, rows, lw), bf16),
            dma((2,)),
            dma((2,)),
            vmem((nh, rows, quarter), bf16),
            vmem((nh, rows, quarter), bf16),
            vmem((nh, rows, quarter), f32),
            dma,
            dma,
        ],
        compiler_params=pltpu.CompilerParams(
            collective_id=0, has_side_effects=True, vmem_limit_bytes=VMEM_MIB * 1024 * 1024
        ),
        name="step",
    )(
        single,
        pair,
        atoms,
        atom_counts.reshape(1, rows),
        jnp.transpose(w_atom, (1, 2, 0)),
        w_atom_token,
        ln_gain,
        jnp.transpose(w_proj, (1, 2, 0)),
        w_pair_bias.T,
        w_out,
        ln_gain2,
        w_trans,
        w_trans_out,
    )
    return pl.pallas_call(
        deliver,
        out_shape=(
            jax.ShapeDtypeStruct((rows, quarter), bf16),
            jax.ShapeDtypeStruct((awidth, slots), bf16),
        ),
        in_specs=[vm, vm],
        out_specs=(hbm, hbm),
        scratch_shapes=[dma((2,))],
        name="deliver",
    )(
        pltpu.with_memory_space_constraint(refined, pltpu.VMEM),
        pltpu.with_memory_space_constraint(atom_mix, pltpu.VMEM),
    )


def solution(mesh):
    return jax.shard_map(
        functools.partial(shards, mesh.shape["tok"], mesh.shape["head"]),
        mesh=mesh,
        in_specs=(
            P("tok", None),
            P("tok", "head", None),
            P("tok", None),
            P("tok"),
            P(None, None, "head"),
            P("head", None),
            P(),
            P(None, None, "head"),
            P(),
            P("head", None),
            P(),
            P(None, None, "head"),
            P("head", None),
        ),
        out_specs=(P("tok", "head"), P("head", "tok")),
        check_vma=False,
    )
```

```python
import functools

import jax
import jax.numpy as jnp
from jax import lax
from jax.experimental import pallas as pl
from jax.experimental.pallas import tpu as pltpu
from jax.sharding import PartitionSpec as P

H = 16
AH = 4
QWIN = 32
KWIN = 128
TAIL = (KWIN - QWIN) // 2
LEAD = (KWIN + QWIN) // 2
MESH = pl.DeviceIdType.MESH
f32 = jnp.float32
bf16 = jnp.bfloat16

norm_eps = 1e-05
masked_value = -1000000000.0
GROUP = 4
FRONT = 2 * QWIN
EDGE = 3
FRONT = 2 * QWIN
EDGE = 3
FRONT = 2 * QWIN
EDGE = 3
FRONT = 2 * QWIN
EDGE = 3
FRONT = 2 * QWIN
EDGE = 3
VMEM_MIB = 58


def dot(a, b):
    return jnp.dot(a, b, preferred_element_type=f32)


def dot_t(a, b):
    return lax.dot_general(a, b, (((1,), (1,)), ((), ())), preferred_element_type=f32)


def iota(shape, dim):
    return lax.broadcasted_iota(jnp.int32, shape, dim)


def eye(n):
    return (iota((n, n), 0) == iota((n, n), 1)).astype(bf16)


def layer_norm(x, gain):
    average = jnp.mean(x, axis=-1, keepdims=True)
    centred = x - average
    spread = jnp.mean(centred * centred, axis=-1, keepdims=True)
    return centred * lax.rsqrt(spread + norm_eps) * gain.astype(f32)


def total_wait(ref, sem):
    pltpu.make_async_copy(ref, ref, sem).wait()


def total_wait(ref, sem):
    pltpu.make_async_copy(ref, ref, sem).wait()


def total_wait(ref, sem):
    pltpu.make_async_copy(ref, ref, sem).wait()


def total_wait(ref, sem):
    pltpu.make_async_copy(ref, ref, sem).wait()


def total_wait(ref, sem):
    pltpu.make_async_copy(ref, ref, sem).wait()


def kernel(
    nt,
    nh,
    single_hbm,
    pair_hbm,
    atoms_hbm,
    counts_hbm,
    w_atom_hbm,
    w_tok_hbm,
    gain1_hbm,
    w_proj_hbm,
    w_pair_hbm,
    w_out_hbm,
    gain2_hbm,
    w_trans_hbm,
    w_down_hbm,
    refined,
    atom_mix,
    counts,
    single,
    atoms,
    w_atom,
    w_tok,
    gain1,
    gain2,
    w_pair,
    pair,
    w_proj,
    w_raw,
    w_gate,
    w_up,
    w_down,
    local_sem,
    relay,
    tail,
    halo,
    halo_s,
    halo_r,
    sg,
    sg_s,
    sg_r,
    fwd_s,
    fwd_r,
    wt,
    wt_s,
    wt_r,
    pair_f,
    pair_s,
    pair_r,
    pb_s,
    pb_r,
    queries,
    keys,
    values,
    inner,
    mixed,
    atoms_in,
    state_in,
    normed_all,
    bias,
    ta,
    ta_s,
    ta_r,
    wo,
    wo_s,
    wo_r,
    gat,
    gat_s,
    gat_r,
    fin_s_buf,
    fin_r_buf,
    own_buf,
    fin_s,
    fin_r,
):
    t = lax.axis_index("tok")
    h = lax.axis_index("head")
    rows, width = single.shape
    slots = atoms.shape[0]
    awidth = w_atom.shape[1]
    heads = w_pair.shape[0]
    local_heads = heads // nh
    lw = w_proj.shape[1]
    hd = lw // local_heads
    kblock = pair.shape[1]
    half = width // 2
    hidden_width = w_gate.shape[1]

    barrier = pltpu.get_barrier_semaphore()
    head_peers = [lax.rem(h + o, nh) for o in range(nh)]

    has_next = t < nt - 1
    has_prev = t > 0
    below = t >= 2
    above = t + 2 < nt
    mate = t + 1 - 2 * lax.rem(t, 2)
    cross = t + 2 * lax.rem(t, 2) - 1
    upper = t + 4 >= nt
    middle = jnp.logical_not(upper) & below
    lower = jnp.logical_not(upper) & jnp.logical_not(below)

    def tell(sem, pt, ph):
        pl.semaphore_signal(sem, inc=1, device_id=(pt, ph), device_id_type=MESH)

    tell(barrier, mate, h)
    pl.when(below & (cross < t))(lambda: tell(barrier, cross, h))
    pl.when(below)(lambda: tell(barrier, t - 2, h))
    for peer in head_peers[1:]:
        tell(barrier, t, peer)
        tell(barrier, mate, peer)

    def tell_later(o, c):
        for peer in head_peers:
            tell(barrier, o, peer)
        return c

    lax.fori_loop(2 * (t // 2) + 2, nt, tell_later, 0)

    def other(o):
        return o + (o - t + nt) // nt

    def everyone(act):
        def step(o, c):
            for peer in head_peers:
                act(other(o), peer)
            return c

        lax.fori_loop(0, nt - 1, step, 0)
        for peer in head_peers[1:]:
            act(t, peer)

    locals_ = [
        pltpu.make_async_copy(src, dst, local_sem.at[i])
        for i, (src, dst) in enumerate(
            [
                (atoms_hbm, atoms),
                (counts_hbm, counts),
                (w_atom_hbm, w_atom),
                (single_hbm, single),
                (w_tok_hbm, w_tok),
                (w_pair_hbm, w_pair),
                (pair_hbm, pair),
                (w_trans_hbm, w_raw),
                (w_proj_hbm, w_proj),
                (gain1_hbm, gain1),
                (w_out_hbm, wo.at[h]),
                (gain2_hbm, gain2),
                (w_down_hbm, w_down),
            ]
        )
    ]
    for copy in locals_:
        copy.start()

    locals_[1].wait()
    cnt_row = counts[...].astype(f32)
    live = jnp.sum(cnt_row, axis=1, keepdims=True).astype(jnp.int32)
    locals_[0].wait()

    @pl.when(has_next)
    def _():
        pick = iota((TAIL, slots), 1) == iota((TAIL, slots), 0) + (live - TAIL)
        tail[...] = dot(pick.astype(bf16), atoms[...]).astype(bf16)

    earlier = (t // 2) * 2 * nh
    some_above = (2 * nt - 3 - t) // nt
    some_cross = lax.rem(t, 2) * ((2 * nt - 2 - t) // nt)
    pl.semaphore_wait(barrier, earlier + 2 * nh - 1 + some_cross + some_above)

    nxt = lax.rem(t + 1, nt)
    prv = lax.rem(t + nt - 1, nt)
    up = pltpu.make_async_remote_copy(
        tail, halo.at[pl.ds(0, TAIL)], halo_s.at[0], halo_r.at[0], device_id=(nxt, h), device_id_type=MESH
    )
    down = pltpu.make_async_remote_copy(
        atoms.at[pl.ds(0, LEAD)],
        halo.at[pl.ds(TAIL, LEAD)],
        halo_s.at[1],
        halo_r.at[1],
        device_id=(prv, h),
        device_id_type=MESH,
    )
    pl.when(has_next)(up.start)
    pl.when(has_prev)(down.start)

    @pl.when(jnp.logical_not(has_prev))
    def _():
        halo[0:TAIL] = jnp.zeros((TAIL, halo.shape[1]), bf16)

    @pl.when(jnp.logical_not(has_next))
    def _():
        halo[TAIL:] = jnp.zeros((LEAD, halo.shape[1]), bf16)


    pl.when(jnp.logical_not(above) & below)(lambda: tell(relay, t - 2, h))

    def hear_above():
        pl.semaphore_wait(relay, 1)
        pl.when(below)(lambda: tell(relay, t - 2, h))

    c_half = lax.rem(h, 2)
    locals_[3].wait()
    locals_[4].wait()
    sg[c_half, pl.ds(pl.multiple_of(t * rows, rows), rows), :] = single[
        :, pl.ds(pl.multiple_of(c_half * half, 128), half)
    ]
    wt[h] = w_tok[...]

    def head_send(src_of, dst, s, r):
        for peer in head_peers[1:]:
            pltpu.make_async_remote_copy(
                src_of(peer), dst.at[h], s, r, device_id=(t, peer), device_id_type=MESH
            ).start()

    def head_wait(ref, sem):
        total_wait(ref.at[pl.ds(0, nh - 1)], sem)

    own_rows = pl.ds(pl.multiple_of(t * rows, rows), rows)

    def start_sg(o, c):
        block = sg.at[c_half, own_rows, :]
        pltpu.make_async_remote_copy(
            block, block, sg_s, sg_r, device_id=(other(o), h), device_id_type=MESH
        ).start()
        return c

    known = 2 * (t // 2) + 1

    def send_single():
        lax.fori_loop(known, nt - 1, start_sg, 0)

    lax.fori_loop(0, known, start_sg, 0)
    head_send(lambda peer: wt.at[h], wt, wt_s, wt_r)

    partner = h + 1 - 2 * c_half
    across = [lax.rem(h + o, nh) for o in range(2, nh, 2)]
    first_part = lw // 4 // 16 * 16

    def give(ref, peer, s, r):
        return pltpu.make_async_remote_copy(ref, ref, s, r, device_id=(t, peer), device_id_type=MESH)

    def give_rows(start, size):
        for peer in across:
            give(wo.at[h, pl.ds(start, size)], peer, wo_s.at[1], wo_r.at[1]).start()


    def give_first():
        locals_[10].wait()
        give_rows(0, first_part)

    pl.when(jnp.logical_not(upper))(give_first)

    ri = iota((rows, rows), 0)
    ci = iota((rows, rows), 1)
    cnt_b = jnp.broadcast_to(cnt_row, (rows, rows))
    cnt_col = jnp.sum(jnp.where(ri == ci, cnt_b, 0.0), axis=1, keepdims=True)
    end_col = jnp.sum(jnp.where(ci <= ri, cnt_b, 0.0), axis=1, keepdims=True)
    end_i = end_col.astype(jnp.int32)
    start_i = (end_col - cnt_col).astype(jnp.int32)
    last = (live - 1) // QWIN
    r0 = (last - (EDGE - 1)) * QWIN

    locals_[2].wait()
    queries[...] = dot_t(atoms[...], w_atom[0]).astype(bf16)
    for ref, i in ((keys, 1), (values, 2)):
        ref[TAIL : TAIL + slots, :awidth] = dot_t(atoms[...], w_atom[i]).astype(bf16)
        ref[0:TAIL, :awidth] = jnp.zeros((TAIL, awidth), bf16)
        ref[TAIL + slots :, :awidth] = jnp.zeros((LEAD, awidth), bf16)
    values[:, awidth:] = jnp.ones((values.shape[0], values.shape[1] - awidth), bf16)

    scale = awidth ** (-0.5)
    qrows = GROUP * QWIN
    krows = qrows + KWIN
    lane = iota((1, krows), 1)
    first = iota((qrows, krows), 0) // QWIN * QWIN
    lanes = iota((qrows, krows), 1)
    band = jnp.where((lanes >= first) & (lanes < first + KWIN), 0.0, masked_value)
    wide_lane = iota((qrows, KWIN), 1)
    for w in range(slots // qrows):
        a = w * qrows
        pos = lane + (a - TAIL)
        outside = jnp.where((pos >= 0) & (pos < live), 0.0, masked_value)
        s = dot_t(queries[a : a + qrows], keys[a : a + krows, :]) * scale + (band + outside)
        top = jnp.max(s, axis=-1, keepdims=True)
        e = jnp.exp(s - top).astype(bf16)
        pv = dot(e, values[a : a + krows, :])
        inner[a : a + qrows] = jnp.where(wide_lane < 2 * awidth, pv, top)
        mixed[a : a + qrows] = (pv[:, :awidth] / pv[:, awidth : awidth + 1]).astype(bf16)

    pl.when(upper & above)(hear_above)
    pl.when(upper & above)(send_single)
    slot = iota((rows, slots), 1)
    member = (slot >= start_i) & (slot < end_i)
    inside = member & (slot >= FRONT) & ((slot < r0) | (slot >= r0 + EDGE * QWIN))
    sums = dot(inside.astype(bf16), mixed[...])
    erow = iota((rows, FRONT + EDGE * QWIN), 1)
    eslot = jnp.where(erow < FRONT, erow, erow - FRONT + r0)
    touched = (eslot >= start_i) & (eslot < end_i) & ((erow < FRONT) | (eslot >= FRONT))
    touched = touched.astype(bf16)

    nrow = FRONT + EDGE * QWIN
    qi = iota((nrow, KWIN), 0)
    ki = iota((nrow, KWIN), 1)
    seen_prev = (qi < FRONT) & (ki < TAIL) & (ki >= qi // QWIN * QWIN) & has_prev
    reach = (qi - FRONT) // QWIN * QWIN + r0 + LEAD - live
    seen_next = (qi >= FRONT) & (ki >= TAIL) & (ki - TAIL < reach) & has_next
    edge_mask = jnp.where(seen_prev | seen_next, 0.0, masked_value)
    pick = iota((EDGE * QWIN, slots), 1) == iota((EDGE * QWIN, slots), 0) + r0
    a_edge = dot(pick.astype(bf16), atoms[...]).astype(bf16)
    a_edge = jnp.concatenate([atoms[0:FRONT], a_edge], axis=0)
    q_edge = dot_t(a_edge, w_atom[0]).astype(bf16)
    q_edge = dot(q_edge, w_atom[1]).astype(bf16)
    in_edge = jnp.dot(pick.astype(f32), inner[...], precision=lax.Precision.HIGHEST, preferred_element_type=f32)
    in_edge = jnp.concatenate([inner[0:FRONT], in_edge], axis=0)
    top_in = in_edge[:, 2 * awidth : 2 * awidth + 1]

    locals_[5].wait()
    locals_[6].wait()
    for i in range(rows):
        pair_f[:, i, :] = dot_t(w_pair[...], pair[i])
    for p in range(nh):
        pair_s[p] = pair_f[p * local_heads : (p + 1) * local_heads].astype(bf16)
    pair_r[h] = pair_s[h]
    head_send(lambda peer: pair_s.at[peer], pair_r, pb_s, pb_r)

    pl.when(middle)(hear_above)
    pl.when(middle)(send_single)
    pl.when(has_prev)(up.wait_recv)
    pl.when(has_next)(down.wait_recv)
    vh = dot_t(halo[...], w_atom[2]).astype(bf16)
    vh = jnp.concatenate([vh, jnp.ones((KWIN, KWIN - awidth), bf16)], axis=1)
    s = dot_t(q_edge, halo[...]) * scale + edge_mask
    top_out = jnp.max(s, axis=-1, keepdims=True)
    e = jnp.exp(s - top_out).astype(bf16)
    pv = dot(e, vh)
    top = jnp.maximum(top_in, top_out)
    pv = jnp.exp(top_in - top) * in_edge + jnp.exp(top_out - top) * pv
    edge = (pv[:, :awidth] / pv[:, awidth : awidth + 1]).astype(bf16)
    means = (sums + dot(touched, edge)) / cnt_col
    packs = KWIN // awidth
    prow = rows // packs
    packed = jnp.concatenate([means[i * prow : (i + 1) * prow] for i in range(packs)], axis=1)
    ta[h, t] = packed.astype(bf16)

    def ta_send(pt, ph):
        block = ta.at[h, t]
        pltpu.make_async_remote_copy(
            block, block, ta_s, ta_r, device_id=(pt, ph), device_id_type=MESH
        ).start()

    pl.when(lower)(hear_above)
    everyone(ta_send)
    pl.when(lower)(send_single)

    locals_[7].wait()
    woven = w_raw[...].reshape(2 * width, hidden_width)
    blk = 128
    si = iota((blk, 2 * blk), 0)
    sj = iota((blk, 2 * blk), 1)
    picks = [(sj == 2 * si + p).astype(bf16) for p in (0, 1)]
    for b in range(width // blk):
        for p, ref in enumerate((w_gate, w_up)):
            ref[b * blk : (b + 1) * blk] = dot(picks[p], woven[2 * b * blk : 2 * (b + 1) * blk]).astype(bf16)

    at_window = iota((QWIN, awidth), 0) // QWIN
    for w in range(slots // QWIN):
        a = w * QWIN
        if a < FRONT:
            mixed[a : a + QWIN] = edge[a : a + QWIN]
        else:
            block = mixed[a : a + QWIN].astype(f32)
            for i in range(EDGE):
                b = FRONT + i * QWIN
                here = at_window + (w + EDGE - 1 - i) == last
                block = jnp.where(here, edge[b : b + QWIN].astype(f32), block)
            mixed[a : a + QWIN] = block.astype(bf16)
    alive = iota((slots, 1), 0) < live
    mix = jnp.where(alive, mixed[...].astype(f32), 0.0).astype(bf16)
    atom_mix[...] = dot_t(eye(awidth), mix).astype(bf16)

    pl.when(upper)(give_first)
    give(wo.at[h], partner, wo_s.at[0], wo_r.at[0]).start()
    give_rows(first_part, lw - first_part)
    total_wait(sg.at[0, pl.ds(0, (nt - 1) * rows), :], sg_r)
    fwd = pltpu.make_async_remote_copy(
        sg.at[c_half], sg.at[c_half], fwd_s, fwd_r, device_id=(t, partner), device_id_type=MESH
    )
    fwd.start()
    head_wait(wt, wt_r)
    head_wait(pair_r, pb_r)
    for i in (8, 9, 11, 12):
        locals_[i].wait()
    bias[...] = jnp.concatenate(
        [pair_r[p].astype(f32).reshape(local_heads * rows, kblock) for p in range(nh)], axis=1
    )
    fwd.wait_recv()
    for i in range(2):
        state_in[:, i * half : (i + 1) * half] = sg[i].astype(f32)
    flat_ta = ta.reshape(nh * nt, prow, packs * awidth).at[pl.ds(0, nh * nt - 1)]
    total_wait(flat_ta, ta_r)

    at_lane = iota((1, packs * awidth), 1)
    blocks = [ta[p].astype(f32).reshape(nt * prow, packs * awidth) for p in range(nh)]
    turned = []
    for i in range(packs):
        block = blocks[0]
        for p in range(nh):
            moved = blocks[p]
            if p != i:
                moved = pltpu.roll(moved, (p - i) % packs * awidth, axis=1)
            block = moved if p == 0 else jnp.where(at_lane >= p * awidth, moved, block)
        turned.append(block.reshape(nt, 1, prow, packs * awidth))
    lhs = jnp.concatenate(turned, axis=1).reshape(nt * rows, packs * awidth).astype(bf16)
    atoms_in[...] = lhs
    w_full = wt[...].reshape(nh * awidth, width)
    normed_all[...] = layer_norm(state_in[...] + dot(lhs, w_full), gain1[...].reshape(1, width)).astype(bf16)
    normed_own = normed_all[own_rows, :]
    q = dot_t(normed_own, w_proj[0])
    k = dot_t(normed_all[...], w_proj[1]).astype(bf16)
    col = iota((1, lw), 1)
    in_head = [(col >= hd * i) & (col < hd * (i + 1)) for i in range(local_heads)]
    stacked = jnp.concatenate([jnp.where(m, q, 0.0) for m in in_head], axis=0).astype(bf16)
    s = dot_t(stacked, k) * hd ** (-0.5)
    v = dot_t(normed_all[...], w_proj[2]).astype(bf16)
    gate = jax.nn.sigmoid(dot_t(normed_own, w_proj[3]))
    s = s + bias[...]
    e = jnp.exp(s - jnp.max(s, axis=-1, keepdims=True))
    ctx = dot(e.astype(bf16), v) / jnp.sum(e, axis=-1, keepdims=True)
    context = jnp.zeros((rows, lw), f32)
    for i, m in enumerate(in_head):
        context = jnp.where(m, ctx[i * rows : (i + 1) * rows], context)
    gated = (context * gate).astype(bf16)
    gat[h] = gated
    for peer in across:
        for far in (peer, peer + 1 - 2 * c_half):
            give(gat.at[h], far, gat_s.at[1], gat_r.at[1]).start()
    give(gat.at[h], partner, gat_s.at[0], gat_r.at[0]).start()
    state = single[...].astype(f32) + dot(atoms_in[own_rows, :], wt[...].reshape(nh * awidth, width))
    n_across = len(across)
    total_wait(wo.at[pl.ds(0, n_across)], wo_r.at[1])
    for peer in across:
        give(wo.at[peer], partner, wo_s.at[2], wo_r.at[2]).start()
    after = state + dot(gated, wo[h])
    total_wait(wo.at[0], wo_r.at[0])
    total_wait(gat.at[0], gat_r.at[0])
    after += dot(gat[partner], wo[partner])

    pl.when(has_next)(up.wait_send)
    pl.when(has_prev)(down.wait_send)
    fwd.wait_send()
    head_wait(wt, wt_s)
    head_wait(pair_r, pb_s)
    total_wait(sg.at[0, pl.ds(0, (nt - 1) * rows), :], sg_s)
    total_wait(flat_ta, ta_s)

    total_wait(wo.at[0], wo_s.at[0])
    total_wait(wo.at[pl.ds(0, n_across)], wo_s.at[1])
    total_wait(wo.at[pl.ds(0, n_across)], wo_r.at[2])
    total_wait(gat.at[pl.ds(0, 2 * n_across)], gat_r.at[1])
    for peer in across:
        for far in (peer, peer + 1 - 2 * c_half):
            after += dot(gat[far], wo[far])
    normed_after = layer_norm(after, gain2[...].reshape(1, width)).astype(bf16)
    g = dot(normed_after, w_gate[...])
    u = dot(normed_after, w_up[...])
    hidden = (jax.nn.silu(g) * u).astype(bf16)
    update = dot(hidden, w_down[...])
    quarter = width // nh
    for p in range(nh):
        fin_s_buf[p] = update[:, p * quarter : (p + 1) * quarter].astype(bf16)
    head_send(lambda peer: fin_s_buf.at[peer], fin_r_buf, fin_s, fin_r)
    for p in range(nh):
        own_buf[p] = after[:, p * quarter : (p + 1) * quarter]
    acc = own_buf[h] + fin_s_buf[h].astype(f32)
    fin_r_buf[h] = jnp.zeros((rows, quarter), bf16)
    total_wait(gat.at[0], gat_s.at[0])
    total_wait(gat.at[pl.ds(0, 2 * n_across)], gat_s.at[1])
    total_wait(wo.at[pl.ds(0, n_across)], wo_s.at[2])
    head_wait(fin_r_buf, fin_s)
    head_wait(fin_r_buf, fin_r)
    for p in range(nh):
        acc += fin_r_buf[p].astype(f32)
    refined[...] = acc.astype(bf16)


def deliver(refined_in, mix_in, refined, atom_mix, sem):
    copies = [
        pltpu.make_async_copy(refined_in, refined, sem.at[0]),
        pltpu.make_async_copy(mix_in, atom_mix, sem.at[1]),
    ]
    for copy in copies:
        copy.start()
    for copy in copies:
        copy.wait()


def shards(
    nt,
    nh,
    single,
    pair,
    atoms,
    atom_counts,
    w_atom,
    w_atom_token,
    ln_gain,
    w_proj,
    w_pair_bias,
    w_out,
    ln_gain2,
    w_trans,
    w_trans_out,
):
    rows, width = single.shape
    slots, channels = atoms.shape
    awidth = w_atom.shape[2]
    heads = w_pair_bias.shape[1]
    local_heads = heads // nh
    kblock = pair.shape[1]
    n = nt * nh
    lw = w_proj.shape[2]
    hidden = w_trans.shape[2]
    quarter = width // nh
    vm = pl.BlockSpec(memory_space=pltpu.VMEM)
    hbm = pl.BlockSpec(memory_space=pltpu.HBM)
    dma = pltpu.SemaphoreType.DMA
    vmem = pltpu.VMEM
    refined, atom_mix = pl.pallas_call(
        functools.partial(kernel, nt, nh),
        out_shape=(vmem((rows, quarter), bf16), vmem((awidth, slots), bf16)),
        in_specs=[hbm] * 13,
        out_specs=(vm, vm),
        scratch_shapes=[
            vmem((1, rows), jnp.int32),
            vmem(single.shape, bf16),
            vmem(atoms.shape, bf16),
            vmem((3, awidth, channels), bf16),
            vmem(w_atom_token.shape, bf16),
            vmem(ln_gain.shape, bf16),
            vmem(ln_gain2.shape, bf16),
            vmem((heads, pair.shape[2]), bf16),
            vmem(pair.shape, bf16),
            vmem((4, lw, width), bf16),
            vmem(w_trans.shape, bf16),
            vmem((width, hidden), bf16),
            vmem((width, hidden), bf16),
            vmem(w_trans_out.shape, bf16),
            dma((13,)),
            pltpu.SemaphoreType.REGULAR,
            vmem((TAIL, channels), bf16),
            vmem((KWIN, channels), bf16),
            dma((2,)),
            dma((2,)),
            vmem((2, nt * rows, width // 2), bf16),
            dma,
            dma,
            dma,
            dma,
            vmem((nh, awidth, width), bf16),
            dma,
            dma,
            vmem((heads, rows, kblock), f32),
            vmem((nh, local_heads, rows, kblock), bf16),
            vmem((nh, local_heads, rows, kblock), bf16),
            dma,
            dma,
            vmem((slots, awidth), bf16),
            vmem((TAIL + slots + LEAD, awidth), bf16),
            vmem((TAIL + slots + LEAD, KWIN), bf16),
            vmem((slots, KWIN), f32),
            vmem((slots, awidth), bf16),
            vmem((nt * rows, nh * awidth), bf16),
            vmem((nt * rows, width), f32),
            vmem((nt * rows, width), bf16),
            vmem((local_heads * rows, nh * kblock), f32),
            vmem((nh, nt, rows * awidth // KWIN, KWIN), bf16),
            dma,
            dma,
            vmem((nh, lw, width), bf16),
            dma((3,)),
            dma((3,)),
            vmem((nh, rows, lw), bf16),
            dma((2,)),
            dma((2,)),
            vmem((nh, rows, quarter), bf16),
            vmem((nh, rows, quarter), bf16),
            vmem((nh, rows, quarter), f32),
            dma,
            dma,
        ],
        compiler_params=pltpu.CompilerParams(
            collective_id=0, has_side_effects=True, vmem_limit_bytes=VMEM_MIB * 1024 * 1024
        ),
        name="step",
    )(
        single,
        pair,
        atoms,
        atom_counts.reshape(1, rows),
        jnp.transpose(w_atom, (1, 2, 0)),
        w_atom_token,
        ln_gain,
        jnp.transpose(w_proj, (1, 2, 0)),
        w_pair_bias.T,
        w_out,
        ln_gain2,
        w_trans,
        w_trans_out,
    )
    return pl.pallas_call(
        deliver,
        out_shape=(
            jax.ShapeDtypeStruct((rows, quarter), bf16),
            jax.ShapeDtypeStruct((awidth, slots), bf16),
        ),
        in_specs=[vm, vm],
        out_specs=(hbm, hbm),
        scratch_shapes=[dma((2,))],
        name="deliver",
    )(
        pltpu.with_memory_space_constraint(refined, pltpu.VMEM),
        pltpu.with_memory_space_constraint(atom_mix, pltpu.VMEM),
    )


def solution(mesh):
    return jax.shard_map(
        functools.partial(shards, mesh.shape["tok"], mesh.shape["head"]),
        mesh=mesh,
        in_specs=(
            P("tok", None),
            P("tok", "head", None),
            P("tok", None),
            P("tok"),
            P(None, None, "head"),
            P("head", None),
            P(),
            P(None, None, "head"),
            P(),
            P("head", None),
            P(),
            P(None, None, "head"),
            P("head", None),
        ),
        out_specs=(P("tok", "head"), P("head", "tok")),
        check_vma=False,
    )
```

```python
import functools

import jax
import jax.numpy as jnp
from jax import lax
from jax.experimental import pallas as pl
from jax.experimental.pallas import tpu as pltpu
from jax.sharding import PartitionSpec as P

H = 16
AH = 4
QWIN = 32
KWIN = 128
TAIL = (KWIN - QWIN) // 2
LEAD = (KWIN + QWIN) // 2
MESH = pl.DeviceIdType.MESH
f32 = jnp.float32
bf16 = jnp.bfloat16

norm_eps = 1e-05
masked_value = -1000000000.0
GROUP = 4
FRONT = 2 * QWIN
EDGE = 3
FRONT = 2 * QWIN
EDGE = 3
FRONT = 2 * QWIN
EDGE = 3
FRONT = 2 * QWIN
EDGE = 3
FRONT = 2 * QWIN
EDGE = 3
VMEM_MIB = 58


def dot(a, b):
    return jnp.dot(a, b, preferred_element_type=f32)


def dot_t(a, b):
    return lax.dot_general(a, b, (((1,), (1,)), ((), ())), preferred_element_type=f32)


def iota(shape, dim):
    return lax.broadcasted_iota(jnp.int32, shape, dim)


def eye(n):
    return (iota((n, n), 0) == iota((n, n), 1)).astype(bf16)


def layer_norm(x, gain):
    average = jnp.mean(x, axis=-1, keepdims=True)
    centred = x - average
    spread = jnp.mean(centred * centred, axis=-1, keepdims=True)
    return centred * lax.rsqrt(spread + norm_eps) * gain.astype(f32)


def total_wait(ref, sem):
    pltpu.make_async_copy(ref, ref, sem).wait()


def total_wait(ref, sem):
    pltpu.make_async_copy(ref, ref, sem).wait()


def total_wait(ref, sem):
    pltpu.make_async_copy(ref, ref, sem).wait()


def total_wait(ref, sem):
    pltpu.make_async_copy(ref, ref, sem).wait()


def total_wait(ref, sem):
    pltpu.make_async_copy(ref, ref, sem).wait()


def kernel(
    nt,
    nh,
    single_hbm,
    pair_hbm,
    atoms_hbm,
    counts_hbm,
    w_atom_hbm,
    w_tok_hbm,
    gain1_hbm,
    w_proj_hbm,
    w_pair_hbm,
    w_out_hbm,
    gain2_hbm,
    w_trans_hbm,
    w_down_hbm,
    refined,
    atom_mix,
    counts,
    single,
    atoms,
    w_atom,
    w_tok,
    gain1,
    gain2,
    w_pair,
    pair,
    w_proj,
    w_raw,
    w_gate,
    w_up,
    w_down,
    local_sem,
    relay,
    tail,
    halo,
    halo_s,
    halo_r,
    sg,
    sg_s,
    sg_r,
    fwd_s,
    fwd_r,
    wt,
    wt_s,
    wt_r,
    pair_f,
    pair_s,
    pair_r,
    pb_s,
    pb_r,
    queries,
    keys,
    values,
    inner,
    mixed,
    atoms_in,
    state_in,
    normed_all,
    bias,
    ta,
    ta_s,
    ta_r,
    wo,
    wo_s,
    wo_r,
    gat,
    gat_s,
    gat_r,
    fin_s_buf,
    fin_r_buf,
    own_buf,
    fin_s,
    fin_r,
):
    t = lax.axis_index("tok")
    h = lax.axis_index("head")
    rows, width = single.shape
    slots = atoms.shape[0]
    awidth = w_atom.shape[1]
    heads = w_pair.shape[0]
    local_heads = heads // nh
    lw = w_proj.shape[1]
    hd = lw // local_heads
    kblock = pair.shape[1]
    half = width // 2
    hidden_width = w_gate.shape[1]

    barrier = pltpu.get_barrier_semaphore()
    head_peers = [lax.rem(h + o, nh) for o in range(nh)]

    has_next = t < nt - 1
    has_prev = t > 0
    below = t >= 2
    above = t + 2 < nt
    mate = t + 1 - 2 * lax.rem(t, 2)
    cross = t + 2 * lax.rem(t, 2) - 1
    upper = t + 4 >= nt
    middle = jnp.logical_not(upper) & below
    lower = jnp.logical_not(upper) & jnp.logical_not(below)

    def tell(sem, pt, ph):
        pl.semaphore_signal(sem, inc=1, device_id=(pt, ph), device_id_type=MESH)

    tell(barrier, mate, h)
    pl.when(below & (cross < t))(lambda: tell(barrier, cross, h))
    pl.when(below)(lambda: tell(barrier, t - 2, h))
    for peer in head_peers[1:]:
        tell(barrier, t, peer)
        tell(barrier, mate, peer)

    def tell_later(o, c):
        for peer in head_peers:
            tell(barrier, o, peer)
        return c

    lax.fori_loop(2 * (t // 2) + 2, nt, tell_later, 0)

    def other(o):
        return o + (o - t + nt) // nt

    def everyone(act):
        def step(o, c):
            for peer in head_peers:
                act(other(o), peer)
            return c

        lax.fori_loop(0, nt - 1, step, 0)
        for peer in head_peers[1:]:
            act(t, peer)

    locals_ = [
        pltpu.make_async_copy(src, dst, local_sem.at[i])
        for i, (src, dst) in enumerate(
            [
                (atoms_hbm, atoms),
                (counts_hbm, counts),
                (w_atom_hbm, w_atom),
                (single_hbm, single),
                (w_tok_hbm, w_tok),
                (w_pair_hbm, w_pair),
                (pair_hbm, pair),
                (w_trans_hbm, w_raw),
                (w_proj_hbm, w_proj),
                (gain1_hbm, gain1),
                (w_out_hbm, wo.at[h]),
                (gain2_hbm, gain2),
                (w_down_hbm, w_down),
            ]
        )
    ]
    for copy in locals_:
        copy.start()

    locals_[1].wait()
    cnt_row = counts[...].astype(f32)
    live = jnp.sum(cnt_row, axis=1, keepdims=True).astype(jnp.int32)
    locals_[0].wait()

    @pl.when(has_next)
    def _():
        pick = iota((TAIL, slots), 1) == iota((TAIL, slots), 0) + (live - TAIL)
        tail[...] = dot(pick.astype(bf16), atoms[...]).astype(bf16)

    earlier = (t // 2) * 2 * nh
    some_above = (2 * nt - 3 - t) // nt
    some_cross = lax.rem(t, 2) * ((2 * nt - 2 - t) // nt)
    pl.semaphore_wait(barrier, earlier + 2 * nh - 1 + some_cross + some_above)

    nxt = lax.rem(t + 1, nt)
    prv = lax.rem(t + nt - 1, nt)
    up = pltpu.make_async_remote_copy(
        tail, halo.at[pl.ds(0, TAIL)], halo_s.at[0], halo_r.at[0], device_id=(nxt, h), device_id_type=MESH
    )
    down = pltpu.make_async_remote_copy(
        atoms.at[pl.ds(0, LEAD)],
        halo.at[pl.ds(TAIL, LEAD)],
        halo_s.at[1],
        halo_r.at[1],
        device_id=(prv, h),
        device_id_type=MESH,
    )
    pl.when(has_next)(up.start)
    pl.when(has_prev)(down.start)

    @pl.when(jnp.logical_not(has_prev))
    def _():
        halo[0:TAIL] = jnp.zeros((TAIL, halo.shape[1]), bf16)

    @pl.when(jnp.logical_not(has_next))
    def _():
        halo[TAIL:] = jnp.zeros((LEAD, halo.shape[1]), bf16)


    pl.when(jnp.logical_not(above) & below)(lambda: tell(relay, t - 2, h))

    def hear_above():
        pl.semaphore_wait(relay, 1)
        pl.when(below)(lambda: tell(relay, t - 2, h))

    c_half = lax.rem(h, 2)
    locals_[3].wait()
    locals_[4].wait()
    sg[c_half, pl.ds(pl.multiple_of(t * rows, rows), rows), :] = single[
        :, pl.ds(pl.multiple_of(c_half * half, 128), half)
    ]
    wt[h] = w_tok[...]

    def head_send(src_of, dst, s, r):
        for peer in head_peers[1:]:
            pltpu.make_async_remote_copy(
                src_of(peer), dst.at[h], s, r, device_id=(t, peer), device_id_type=MESH
            ).start()

    def head_wait(ref, sem):
        total_wait(ref.at[pl.ds(0, nh - 1)], sem)

    own_rows = pl.ds(pl.multiple_of(t * rows, rows), rows)

    def start_sg(o, c):
        block = sg.at[c_half, own_rows, :]
        pltpu.make_async_remote_copy(
            block, block, sg_s, sg_r, device_id=(other(o), h), device_id_type=MESH
        ).start()
        return c

    known = 2 * (t // 2) + 1

    def send_single():
        lax.fori_loop(known, nt - 1, start_sg, 0)

    lax.fori_loop(0, known, start_sg, 0)
    head_send(lambda peer: wt.at[h], wt, wt_s, wt_r)

    partner = h + 1 - 2 * c_half
    across = [lax.rem(h + o, nh) for o in range(2, nh, 2)]
    first_part = lw // 4 // 16 * 16

    def give(ref, peer, s, r):
        return pltpu.make_async_remote_copy(ref, ref, s, r, device_id=(t, peer), device_id_type=MESH)

    def give_rows(start, size):
        for peer in across:
            give(wo.at[h, pl.ds(start, size)], peer, wo_s.at[1], wo_r.at[1]).start()


    def give_first():
        locals_[10].wait()
        give_rows(0, first_part)

    pl.when(jnp.logical_not(upper))(give_first)

    ri = iota((rows, rows), 0)
    ci = iota((rows, rows), 1)
    cnt_b = jnp.broadcast_to(cnt_row, (rows, rows))
    cnt_col = jnp.sum(jnp.where(ri == ci, cnt_b, 0.0), axis=1, keepdims=True)
    end_col = jnp.sum(jnp.where(ci <= ri, cnt_b, 0.0), axis=1, keepdims=True)
    end_i = end_col.astype(jnp.int32)
    start_i = (end_col - cnt_col).astype(jnp.int32)
    last = (live - 1) // QWIN
    r0 = (last - (EDGE - 1)) * QWIN

    locals_[2].wait()
    queries[...] = dot_t(atoms[...], w_atom[0]).astype(bf16)
    for ref, i in ((keys, 1), (values, 2)):
        ref[TAIL : TAIL + slots, :awidth] = dot_t(atoms[...], w_atom[i]).astype(bf16)
        ref[0:TAIL, :awidth] = jnp.zeros((TAIL, awidth), bf16)
        ref[TAIL + slots :, :awidth] = jnp.zeros((LEAD, awidth), bf16)
    values[:, awidth:] = jnp.ones((values.shape[0], values.shape[1] - awidth), bf16)

    scale = awidth ** (-0.5)
    qrows = GROUP * QWIN
    krows = qrows + KWIN
    lane = iota((1, krows), 1)
    first = iota((qrows, krows), 0) // QWIN * QWIN
    lanes = iota((qrows, krows), 1)
    band = jnp.where((lanes >= first) & (lanes < first + KWIN), 0.0, masked_value)
    wide_lane = iota((qrows, KWIN), 1)
    for w in range(slots // qrows):
        a = w * qrows
        pos = lane + (a - TAIL)
        outside = jnp.where((pos >= 0) & (pos < live), 0.0, masked_value)
        s = dot_t(queries[a : a + qrows], keys[a : a + krows, :]) * scale + (band + outside)
        top = jnp.max(s, axis=-1, keepdims=True)
        e = jnp.exp(s - top).astype(bf16)
        pv = dot(e, values[a : a + krows, :])
        inner[a : a + qrows] = jnp.where(wide_lane < 2 * awidth, pv, top)
        mixed[a : a + qrows] = (pv[:, :awidth] / pv[:, awidth : awidth + 1]).astype(bf16)

    pl.when(upper & above)(hear_above)
    pl.when(upper & above)(send_single)
    slot = iota((rows, slots), 1)
    member = (slot >= start_i) & (slot < end_i)
    inside = member & (slot >= FRONT) & ((slot < r0) | (slot >= r0 + EDGE * QWIN))
    sums = dot(inside.astype(bf16), mixed[...])
    erow = iota((rows, FRONT + EDGE * QWIN), 1)
    eslot = jnp.where(erow < FRONT, erow, erow - FRONT + r0)
    touched = (eslot >= start_i) & (eslot < end_i) & ((erow < FRONT) | (eslot >= FRONT))
    touched = touched.astype(bf16)

    nrow = FRONT + EDGE * QWIN
    qi = iota((nrow, KWIN), 0)
    ki = iota((nrow, KWIN), 1)
    seen_prev = (qi < FRONT) & (ki < TAIL) & (ki >= qi // QWIN * QWIN) & has_prev
    reach = (qi - FRONT) // QWIN * QWIN + r0 + LEAD - live
    seen_next = (qi >= FRONT) & (ki >= TAIL) & (ki - TAIL < reach) & has_next
    edge_mask = jnp.where(seen_prev | seen_next, 0.0, masked_value)
    pick = iota((EDGE * QWIN, slots), 1) == iota((EDGE * QWIN, slots), 0) + r0
    a_edge = dot(pick.astype(bf16), atoms[...]).astype(bf16)
    a_edge = jnp.concatenate([atoms[0:FRONT], a_edge], axis=0)
    q_edge = dot_t(a_edge, w_atom[0]).astype(bf16)
    in_edge = jnp.dot(pick.astype(f32), inner[...], precision=lax.Precision.HIGHEST, preferred_element_type=f32)
    in_edge = jnp.concatenate([inner[0:FRONT], in_edge], axis=0)
    top_in = in_edge[:, 2 * awidth : 2 * awidth + 1]

    locals_[5].wait()
    locals_[6].wait()
    for i in range(rows):
        pair_f[:, i, :] = dot_t(w_pair[...], pair[i])
    for p in range(nh):
        pair_s[p] = pair_f[p * local_heads : (p + 1) * local_heads].astype(bf16)
    pair_r[h] = pair_s[h]
    head_send(lambda peer: pair_s.at[peer], pair_r, pb_s, pb_r)

    pl.when(middle)(hear_above)
    pl.when(middle)(send_single)
    pl.when(has_prev)(up.wait_recv)
    pl.when(has_next)(down.wait_recv)
    kh = dot_t(halo[...], w_atom[1]).astype(bf16)
    vh = dot_t(halo[...], w_atom[2]).astype(bf16)
    vh = jnp.concatenate([vh, jnp.ones((KWIN, KWIN - awidth), bf16)], axis=1)
    s = dot_t(q_edge, kh) * scale + edge_mask
    top_out = jnp.max(s, axis=-1, keepdims=True)
    e = jnp.exp(s - top_out).astype(bf16)
    pv = dot(e, vh)
    top = jnp.maximum(top_in, top_out)
    pv = jnp.exp(top_in - top) * in_edge + jnp.exp(top_out - top) * pv
    edge = (pv[:, :awidth] / pv[:, awidth : awidth + 1]).astype(bf16)
    means = (sums + dot(touched, edge)) / cnt_col
    packs = KWIN // awidth
    prow = rows // packs
    packed = jnp.concatenate([means[i * prow : (i + 1) * prow] for i in range(packs)], axis=1)
    ta[h, t] = packed.astype(bf16)

    def ta_send(pt, ph):
        block = ta.at[h, t]
        pltpu.make_async_remote_copy(
            block, block, ta_s, ta_r, device_id=(pt, ph), device_id_type=MESH
        ).start()

    pl.when(lower)(hear_above)
    everyone(ta_send)
    pl.when(lower)(send_single)

    locals_[7].wait()
    woven = w_raw[...].reshape(2 * width, hidden_width)
    blk = 128
    si = iota((blk, 2 * blk), 0)
    sj = iota((blk, 2 * blk), 1)
    picks = [(sj == 2 * si + p).astype(bf16) for p in (0, 1)]
    for b in range(width // blk):
        for p, ref in enumerate((w_gate, w_up)):
            ref[b * blk : (b + 1) * blk] = dot(picks[p], woven[2 * b * blk : 2 * (b + 1) * blk]).astype(bf16)

    at_window = iota((QWIN, awidth), 0) // QWIN
    for w in range(slots // QWIN):
        a = w * QWIN
        if a < FRONT:
            mixed[a : a + QWIN] = edge[a : a + QWIN]
        else:
            block = mixed[a : a + QWIN].astype(f32)
            for i in range(EDGE):
                b = FRONT + i * QWIN
                here = at_window + (w + EDGE - 1 - i) == last
                block = jnp.where(here, edge[b : b + QWIN].astype(f32), block)
            mixed[a : a + QWIN] = block.astype(bf16)
    alive = iota((slots, 1), 0) < live
    mix = jnp.where(alive, mixed[...].astype(f32), 0.0).astype(bf16)
    atom_mix[...] = dot_t(eye(awidth), mix).astype(bf16)

    pl.when(upper)(give_first)
    give(wo.at[h], partner, wo_s.at[0], wo_r.at[0]).start()
    give_rows(first_part, lw - first_part)
    total_wait(sg.at[0, pl.ds(0, (nt - 1) * rows), :], sg_r)
    fwd = pltpu.make_async_remote_copy(
        sg.at[c_half], sg.at[c_half], fwd_s, fwd_r, device_id=(t, partner), device_id_type=MESH
    )
    fwd.start()
    head_wait(wt, wt_r)
    head_wait(pair_r, pb_r)
    for i in (8, 9, 11, 12):
        locals_[i].wait()
    bias[...] = jnp.concatenate(
        [pair_r[p].astype(f32).reshape(local_heads * rows, kblock) for p in range(nh)], axis=1
    )
    fwd.wait_recv()
    for i in range(2):
        state_in[:, i * half : (i + 1) * half] = sg[i].astype(f32)
    flat_ta = ta.reshape(nh * nt, prow, packs * awidth).at[pl.ds(0, nh * nt - 1)]
    total_wait(flat_ta, ta_r)

    at_lane = iota((1, packs * awidth), 1)
    blocks = [ta[p].astype(f32).reshape(nt * prow, packs * awidth) for p in range(nh)]
    turned = []
    for i in range(packs):
        block = blocks[0]
        for p in range(nh):
            moved = blocks[p]
            if p != i:
                moved = pltpu.roll(moved, (p - i) % packs * awidth, axis=1)
            block = moved if p == 0 else jnp.where(at_lane >= p * awidth, moved, block)
        turned.append(block.reshape(nt, 1, prow, packs * awidth))
    lhs = jnp.concatenate(turned, axis=1).reshape(nt * rows, packs * awidth).astype(bf16)
    atoms_in[...] = lhs
    w_full = wt[...].reshape(nh * awidth, width)
    normed_all[...] = layer_norm(state_in[...] + dot(lhs, w_full), gain1[...].reshape(1, width)).astype(bf16)
    normed_own = normed_all[own_rows, :]
    q = dot_t(normed_own, w_proj[0])
    k = dot_t(normed_all[...], w_proj[1]).astype(bf16)
    col = iota((1, lw), 1)
    in_head = [(col >= hd * i) & (col < hd * (i + 1)) for i in range(local_heads)]
    stacked = jnp.concatenate([jnp.where(m, q, 0.0) for m in in_head], axis=0).astype(bf16)
    s = dot_t(stacked, k) * hd ** (-0.5)
    v = dot_t(normed_all[...], w_proj[2]).astype(bf16)
    gate = jax.nn.sigmoid(dot_t(normed_own, w_proj[3]))
    s = s + bias[...]
    e = jnp.exp(s - jnp.max(s, axis=-1, keepdims=True))
    ctx = dot(e.astype(bf16), v) / jnp.sum(e, axis=-1, keepdims=True)
    context = jnp.zeros((rows, lw), f32)
    for i, m in enumerate(in_head):
        context = jnp.where(m, ctx[i * rows : (i + 1) * rows], context)
    gated = (context * gate).astype(bf16)
    gat[h] = gated
    for peer in across:
        for far in (peer, peer + 1 - 2 * c_half):
            give(gat.at[h], far, gat_s.at[1], gat_r.at[1]).start()
    give(gat.at[h], partner, gat_s.at[0], gat_r.at[0]).start()
    state = single[...].astype(f32) + dot(atoms_in[own_rows, :], wt[...].reshape(nh * awidth, width))
    n_across = len(across)
    total_wait(wo.at[pl.ds(0, n_across)], wo_r.at[1])
    for peer in across:
        give(wo.at[peer], partner, wo_s.at[2], wo_r.at[2]).start()
    after = state + dot(gated, wo[h])
    total_wait(wo.at[0], wo_r.at[0])
    total_wait(gat.at[0], gat_r.at[0])
    after += dot(gat[partner], wo[partner])

    pl.when(has_next)(up.wait_send)
    pl.when(has_prev)(down.wait_send)
    fwd.wait_send()
    head_wait(wt, wt_s)
    head_wait(pair_r, pb_s)
    total_wait(sg.at[0, pl.ds(0, (nt - 1) * rows), :], sg_s)
    total_wait(flat_ta, ta_s)

    total_wait(wo.at[0], wo_s.at[0])
    total_wait(wo.at[pl.ds(0, n_across)], wo_s.at[1])
    total_wait(wo.at[pl.ds(0, n_across)], wo_r.at[2])
    total_wait(gat.at[pl.ds(0, 2 * n_across)], gat_r.at[1])
    for peer in across:
        for far in (peer, peer + 1 - 2 * c_half):
            after += dot(gat[far], wo[far])
    normed_after = layer_norm(after, gain2[...].reshape(1, width)).astype(bf16)
    g = dot(normed_after, w_gate[...])
    u = dot(normed_after, w_up[...])
    hidden = (jax.nn.silu(g) * u).astype(bf16)
    update = dot(hidden, w_down[...])
    quarter = width // nh
    for p in range(nh):
        fin_s_buf[p] = update[:, p * quarter : (p + 1) * quarter].astype(bf16)
    head_send(lambda peer: fin_s_buf.at[peer], fin_r_buf, fin_s, fin_r)
    for p in range(nh):
        own_buf[p] = after[:, p * quarter : (p + 1) * quarter]
    acc = own_buf[h] + fin_s_buf[h].astype(f32)
    fin_r_buf[h] = jnp.zeros((rows, quarter), bf16)
    total_wait(gat.at[0], gat_s.at[0])
    total_wait(gat.at[pl.ds(0, 2 * n_across)], gat_s.at[1])
    total_wait(wo.at[pl.ds(0, n_across)], wo_s.at[2])
    head_wait(fin_r_buf, fin_s)
    head_wait(fin_r_buf, fin_r)
    for p in range(nh):
        acc += fin_r_buf[p].astype(f32)
    refined[...] = acc.astype(bf16)


def deliver(refined_in, mix_in, refined, atom_mix, sem):
    copies = [
        pltpu.make_async_copy(refined_in, refined, sem.at[0]),
        pltpu.make_async_copy(mix_in, atom_mix, sem.at[1]),
    ]
    for copy in copies:
        copy.start()
    for copy in copies:
        copy.wait()


def shards(
    nt,
    nh,
    single,
    pair,
    atoms,
    atom_counts,
    w_atom,
    w_atom_token,
    ln_gain,
    w_proj,
    w_pair_bias,
    w_out,
    ln_gain2,
    w_trans,
    w_trans_out,
):
    rows, width = single.shape
    slots, channels = atoms.shape
    awidth = w_atom.shape[2]
    heads = w_pair_bias.shape[1]
    local_heads = heads // nh
    kblock = pair.shape[1]
    n = nt * nh
    lw = w_proj.shape[2]
    hidden = w_trans.shape[2]
    quarter = width // nh
    vm = pl.BlockSpec(memory_space=pltpu.VMEM)
    hbm = pl.BlockSpec(memory_space=pltpu.HBM)
    dma = pltpu.SemaphoreType.DMA
    vmem = pltpu.VMEM
    refined, atom_mix = pl.pallas_call(
        functools.partial(kernel, nt, nh),
        out_shape=(vmem((rows, quarter), bf16), vmem((awidth, slots), bf16)),
        in_specs=[hbm] * 13,
        out_specs=(vm, vm),
        scratch_shapes=[
            vmem((1, rows), jnp.int32),
            vmem(single.shape, bf16),
            vmem(atoms.shape, bf16),
            vmem((3, awidth, channels), bf16),
            vmem(w_atom_token.shape, bf16),
            vmem(ln_gain.shape, bf16),
            vmem(ln_gain2.shape, bf16),
            vmem((heads, pair.shape[2]), bf16),
            vmem(pair.shape, bf16),
            vmem((4, lw, width), bf16),
            vmem(w_trans.shape, bf16),
            vmem((width, hidden), bf16),
            vmem((width, hidden), bf16),
            vmem(w_trans_out.shape, bf16),
            dma((13,)),
            pltpu.SemaphoreType.REGULAR,
            vmem((TAIL, channels), bf16),
            vmem((KWIN, channels), bf16),
            dma((2,)),
            dma((2,)),
            vmem((2, nt * rows, width // 2), bf16),
            dma,
            dma,
            dma,
            dma,
            vmem((nh, awidth, width), bf16),
            dma,
            dma,
            vmem((heads, rows, kblock), f32),
            vmem((nh, local_heads, rows, kblock), bf16),
            vmem((nh, local_heads, rows, kblock), bf16),
            dma,
            dma,
            vmem((slots, awidth), bf16),
            vmem((TAIL + slots + LEAD, awidth), bf16),
            vmem((TAIL + slots + LEAD, KWIN), bf16),
            vmem((slots, KWIN), f32),
            vmem((slots, awidth), bf16),
            vmem((nt * rows, nh * awidth), bf16),
            vmem((nt * rows, width), f32),
            vmem((nt * rows, width), bf16),
            vmem((local_heads * rows, nh * kblock), f32),
            vmem((nh, nt, rows * awidth // KWIN, KWIN), bf16),
            dma,
            dma,
            vmem((nh, lw, width), bf16),
            dma((3,)),
            dma((3,)),
            vmem((nh, rows, lw), bf16),
            dma((2,)),
            dma((2,)),
            vmem((nh, rows, quarter), bf16),
            vmem((nh, rows, quarter), bf16),
            vmem((nh, rows, quarter), f32),
            dma,
            dma,
        ],
        compiler_params=pltpu.CompilerParams(
            collective_id=0, has_side_effects=True, vmem_limit_bytes=VMEM_MIB * 1024 * 1024
        ),
        name="step",
    )(
        single,
        pair,
        atoms,
        atom_counts.reshape(1, rows),
        jnp.transpose(w_atom, (1, 2, 0)),
        w_atom_token,
        ln_gain,
        jnp.transpose(w_proj, (1, 2, 0)),
        w_pair_bias.T,
        w_out,
        ln_gain2,
        w_trans,
        w_trans_out,
    )
    return pl.pallas_call(
        deliver,
        out_shape=(
            jax.ShapeDtypeStruct((rows, quarter), bf16),
            jax.ShapeDtypeStruct((awidth, slots), bf16),
        ),
        in_specs=[vm, vm],
        out_specs=(hbm, hbm),
        scratch_shapes=[dma((2,))],
        name="deliver",
    )(
        pltpu.with_memory_space_constraint(refined, pltpu.VMEM),
        pltpu.with_memory_space_constraint(atom_mix, pltpu.VMEM),
    )


def solution(mesh):
    return jax.shard_map(
        functools.partial(shards, mesh.shape["tok"], mesh.shape["head"]),
        mesh=mesh,
        in_specs=(
            P("tok", None),
            P("tok", "head", None),
            P("tok", None),
            P("tok"),
            P(None, None, "head"),
            P("head", None),
            P(),
            P(None, None, "head"),
            P(),
            P("head", None),
            P(),
            P(None, None, "head"),
            P("head", None),
        ),
        out_specs=(P("tok", "head"), P("head", "tok")),
        check_vma=False,
    )
```
